32 devices in a mesh: band: 8 (over z, x), lon: 4 (over y, core).
Axes of the slice: x: 2, y: 2, z: 4, core: 2. Of those that a mesh axis runs over, the one named last changes fastest.
Arguments:
- coefficients: bfloat16 [8, 640, 4, 64], P('lon', 'band'), may hold values from -6 to 6
- cycle_length: int32 [64], replicated, may hold values from 20 to 5136, as said below
- row_latitude: int32 [64], replicated, may hold values from 0 to 63, each once
- pair_band: int32 [640], replicated, may hold values from 0 to 7, as said below
- gridpoint_factor: bfloat16 [64, 5632], P('band', 'lon'), may hold values from 0.5 to 2
Outputs:
- grid_values: bfloat16 [8, 64, 5632], P(None, 'band', 'lon')
- tendencies: bfloat16 [8, 640, 4, 64], P('lon', 'band')
The draws below stay inside these ranges and needn't reach their ends.
Inputs may be any that keep to these rules, and one draw needn't show every extreme that they name: `cycle_length`: each entry is 20 + 4 i for a whole number i; some entry equals 5136. `pair_band`: each band owns at most 80 pairs and some band owns exactly that many. `row_latitude`: each latitude appears once.
All inputs are finite; a program needn't handle non-finite values.
Results may differ from the reference program's by a relative error of at most 0.0068.
Values may be sent and summed in bfloat16 or wider, within the bound.
A program may use at most 128 MiB of HBM per device.

```python
import math
import jax
import jax.numpy as jnp
from jax import lax

M = 1280
FIELD_LEVELS = 8
LATITUDE_ROWS = 64
PAIR_SLOTS = 80
SLOT_TOTAL = 640
PTS_DEV = 1408
NPTS = 5632
N_BAND = 8
N_LON = 4


def draw_cycle_length(key, part):
    cycle_steps = jax.random.randint(jax.random.fold_in(key, 11), (LATITUDE_ROWS,), 0, M)
    widest = jax.random.randint(jax.random.fold_in(key, 12), (), 0, LATITUDE_ROWS)
    cycle_steps = cycle_steps.at[widest].set(M - 1)
    return (20 + 4 * cycle_steps).astype(jnp.int32)


def draw_pair_band(key, part):
    shuffled = jax.random.permutation(jax.random.fold_in(key, 21), M // 2)
    relabel = jax.random.permutation(jax.random.fold_in(key, 22), N_BAND)
    return relabel[shuffled % N_BAND].astype(jnp.int32)


def steps_of(stream_key, extent, shards, low, largest):
    loudness, own = 1.0, jax.random.fold_in(stream_key, 6)
    for dim, blocks in shards:
        heights = jnp.exp(jax.random.uniform(jax.random.fold_in(own, dim), (blocks,), jnp.float32, low / len(shards), largest / len(shards)))
        loudness = loudness * jnp.repeat(heights, extent[dim] // blocks).reshape([-1 if axis == dim else 1 for axis in range(len(extent))])
    return loudness


def scatter_about(stream_key, dims, deviation, bound, cuts=(), held_as=jnp.bfloat16):
    loudness = steps_of(stream_key, dims, cuts, -0.22, 0.18) if cuts else 1.0
    values = jax.random.normal(stream_key, dims, jnp.float32) * deviation * loudness
    return jnp.minimum(jnp.maximum(values, -bound), bound).astype(held_as)


def setup_inputs(seed: int = 0) -> dict:
    key_of = jax.random.split(jax.random.key(seed), 6)
    coefficients = scatter_about(key_of[0], (FIELD_LEVELS, SLOT_TOTAL, 4, LATITUDE_ROWS), 1.0, 6.0, ((0, 4), (1, 8)))
    cycle_length = draw_cycle_length(jax.random.fold_in(key_of[5], 71), 0)
    row_latitude = jax.random.permutation(key_of[2], LATITUDE_ROWS).astype(jnp.int32)
    pair_band = draw_pair_band(jax.random.fold_in(key_of[5], 71), 0)
    gridpoint_factor = jnp.clip(jnp.exp(math.log(2.0) - 1.3862944 * jax.random.uniform(key_of[4], (LATITUDE_ROWS, NPTS), jnp.float32) ** steps_of(key_of[4], (LATITUDE_ROWS, NPTS), ((0, 8), (1, 4)), -0.2, 0.2)), 0.5, 2.0).astype(jnp.bfloat16)
    return dict(coefficients=coefficients, cycle_length=cycle_length, row_latitude=row_latitude, pair_band=pair_band, gridpoint_factor=gridpoint_factor)


TWO_PI = 2.0 * math.pi

def slot_maps(pair_band, band_count, slot_count, wave_count):
    pair_count = pair_band.shape[0]
    onehot = (pair_band[:, None] == jnp.arange(band_count, dtype=jnp.int32)[None, :]).astype(jnp.int32)
    before = jnp.cumsum(onehot, axis=0).astype(jnp.int32) - onehot
    position_within_band = lax.optimization_barrier(jnp.sum(before * onehot, axis=1)).astype(jnp.int32)
    slot_of_pair = (pair_band * slot_count + position_within_band).astype(jnp.int32)
    slot_of_wave = jnp.concatenate([slot_of_pair, slot_of_pair[::-1]]).astype(jnp.int32)
    member_of_wave = (jnp.arange(wave_count, dtype=jnp.int32) >= pair_count).astype(jnp.int32)
    pair_of_slot = jnp.full((band_count * slot_count,), -1, jnp.int32).at[slot_of_pair].set(jnp.arange(pair_count, dtype=jnp.int32))
    occupied = pair_of_slot >= 0
    first_wave = jnp.where(occupied, pair_of_slot, 0).astype(jnp.int32)
    wave_of_slot = jnp.stack([first_wave, wave_count - 1 - first_wave], axis=1).astype(jnp.int32)
    return (slot_of_wave, member_of_wave, wave_of_slot, occupied)

def cycle_table(lengths, wave_count, points):
    places = jnp.arange(points, dtype=jnp.int32)
    low_index = jnp.arange(32, dtype=jnp.int32)
    high_index = 32 * jnp.arange(wave_count // 32, dtype=jnp.int32)

    def single_period(length):
        scale = TWO_PI / length.astype(jnp.float32)
        fine = (low_index[:, None] * places[None, :] % length).astype(jnp.float32) * scale
        coarse = (high_index[:, None] * places[None, :] % length).astype(jnp.float32) * scale
        cos_fine, sin_fine = (jnp.cos(fine), jnp.sin(fine))
        cos_coarse, sin_coarse = (jnp.cos(coarse), jnp.sin(coarse))
        cosine = cos_coarse[:, None, :] * cos_fine[None] - sin_coarse[:, None, :] * sin_fine[None]
        sine = sin_coarse[:, None, :] * cos_fine[None] + cos_coarse[:, None, :] * sin_fine[None]
        return jnp.stack([cosine.reshape(wave_count, points), -sine.reshape(wave_count, points)]).astype(jnp.bfloat16)
    return lax.map(single_period, lengths)

def turn_factors(lengths, wave_count, offsets):
    wave_index = jnp.arange(wave_count, dtype=jnp.int32)
    turn_count = offsets[:, None, None] * wave_index[None, None, :] % lengths[None, :, None]
    angles = turn_count.astype(jnp.float32) * (TWO_PI / lengths.astype(jnp.float32))[None, :, None]
    return (jnp.cos(angles), jnp.sin(angles))

def kept_mask(lengths, wave_count):
    wave_index = jnp.arange(wave_count, dtype=jnp.int32)
    return (2 * wave_index[None, :] < lengths[:, None]).astype(jnp.float32)

def weighted(fourier, lengths):
    wave_count = fourier.shape[3]
    wave_index = jnp.arange(wave_count, dtype=jnp.int32)
    doubled = jnp.where(wave_index == 0, 1.0, 2.0).astype(jnp.float32)
    factor = doubled[None, :] * kept_mask(lengths, wave_count) * lax.rsqrt(lengths.astype(jnp.float32))[:, None]
    return fourier.astype(jnp.float32) * factor[None, :, None, :]

def turned(scaled, cosines, sine_values):
    real_part = scaled[:, None, :, 0, :]
    imag_part = scaled[:, None, :, 1, :]
    new_real = real_part * cosines[None] - imag_part * sine_values[None]
    new_imag = real_part * sine_values[None] + imag_part * cosines[None]
    return jnp.stack([new_real, new_imag], axis=3).astype(jnp.bfloat16)

def synthesize(coeffs, tables, lengths, offsets):
    values = jnp.einsum('fdrtm,rtml->frdl', coeffs.astype(jnp.float32), tables.astype(jnp.float32))
    places = offsets[None, :, None] + jnp.arange(tables.shape[3], dtype=jnp.int32)[None, None, :]
    inside = places < lengths[:, None, None]
    return jnp.where(inside[None], values, 0.0).astype(jnp.bfloat16)

def analyze(values, tables):
    return jnp.einsum('frdl,rtml->fdrtm', values.astype(jnp.float32), tables.astype(jnp.float32))

def untwist(partials, cosines, sine_values):
    real_part = partials[:, :, :, 0, :]
    imag_part = partials[:, :, :, 1, :]
    new_real = lax.optimization_barrier(jnp.sum(real_part * cosines[None] + imag_part * sine_values[None], axis=1))
    new_imag = lax.optimization_barrier(jnp.sum(imag_part * cosines[None] - real_part * sine_values[None], axis=1))
    return jnp.stack([new_real, new_imag], axis=2)

def finish(summed, lengths):
    wave_count = summed.shape[3]
    factor = kept_mask(lengths, wave_count) * lax.rsqrt(lengths.astype(jnp.float32))[:, None]
    return (summed * factor[None, :, None, :]).astype(jnp.bfloat16)

def reference(coefficients, cycle_length, row_latitude, pair_band, gridpoint_factor):
    slot_of_wave, member_of_wave, wave_of_slot, occupied = slot_maps(pair_band, N_BAND, PAIR_SLOTS, M)
    split_view = coefficients.reshape(FIELD_LEVELS, N_BAND * PAIR_SLOTS, 2, 2, LATITUDE_ROWS)
    picked = split_view[:, slot_of_wave, member_of_wave]
    offsets = (PTS_DEV * jnp.arange(N_LON, dtype=jnp.int32)).astype(jnp.int32)

    def one_row(row_number):
        latitude_value = row_latitude[row_number]
        lengths = jnp.take(cycle_length, latitude_value[None])
        fourier = jnp.transpose(jnp.take(picked, latitude_value[None], axis=3), (0, 3, 2, 1))
        tables = cycle_table(lengths, M, PTS_DEV)
        cosines, sine_values = turn_factors(lengths, M, offsets)
        coeffs = turned(weighted(fourier, lengths), cosines, sine_values)
        blocks = synthesize(coeffs, tables, lengths, offsets)
        factor_row = lax.dynamic_slice_in_dim(gridpoint_factor, row_number, 1, 0)
        products = (factor_row.astype(jnp.float32).reshape(1, 1, N_LON, PTS_DEV) * blocks.astype(jnp.float32)).astype(jnp.bfloat16)
        summed = untwist(analyze(products, tables), cosines, sine_values)
        return (blocks.reshape(FIELD_LEVELS, NPTS), finish(summed, lengths)[:, 0])
    grid_rows, spectral_rows = lax.map(one_row, jnp.arange(LATITUDE_ROWS, dtype=jnp.int32))
    grid_values = jnp.transpose(grid_rows, (1, 0, 2))
    inverse_rows = jnp.zeros((LATITUDE_ROWS,), jnp.int32).at[row_latitude].set(jnp.arange(LATITUDE_ROWS, dtype=jnp.int32))
    by_latitude = jnp.transpose(jnp.take(spectral_rows, inverse_rows, axis=0), (1, 3, 2, 0))
    placed = by_latitude[:, wave_of_slot]
    placed = jnp.where(occupied[None, :, None, None, None], placed, jnp.zeros_like(placed))
    tendencies = placed.reshape(FIELD_LEVELS, N_BAND * PAIR_SLOTS, 4, LATITUDE_ROWS)
    return (grid_values, tendencies)
```

```python
import functools
import math

import jax
import jax.numpy as jnp
import numpy as np
from jax import lax
from jax.experimental import pallas as pl
from jax.experimental.pallas import tpu as pltpu
from jax.sharding import PartitionSpec as P

TWO_PI = 2.0 * math.pi
LANES = 128
CHUNK = 256
GROUP = 64
MESH = pl.DeviceIdType.MESH


def cos_sin(product, length, inverse):
    turns = jnp.floor(product * inverse + 0.5)
    half = (product - turns * length) * (inverse * (0.5 * TWO_PI))
    square = half * half
    sine = jnp.full_like(half, -1.0 / math.factorial(11))
    for order in (9, 7, 5, 3, 1):
        sine = sine * square + (-1.0) ** (order // 2) / math.factorial(order)
    sine = sine * half
    cosine = jnp.full_like(half, 1.0 / math.factorial(12))
    for order in (10, 8, 6, 4, 2, 0):
        cosine = cosine * square + (-1.0) ** (order // 2) / math.factorial(order)
    return 1.0 - 2.0 * sine * sine, 2.0 * sine * cosine


def round_kernel(
    bands,
    lanes,
    coefficients_hbm,
    cycle_hbm,
    latitude_hbm,
    pair_band_hbm,
    factor_hbm,
    order_hbm,
    blocks,
    tendencies,
    coefficients,
    cycle_ref,
    latitude_ref,
    pair_band_ref,
    factor_ref,
    order_ref,
    pick,
    leaving,
    arrived,
    result,
    returned,
    cycles,
    grid_ref,
    table,
    lhs,
    product_ref,
    row_factor,
    wave_column,
    step_ref,
    weight_ref,
    finished,
    input_sem,
    send_sem,
    recv_sem,
    back_send_sem,
    back_recv_sem,
    factor_send_sem,
    factor_recv_sem,
    grid_send_sem,
    grid_recv_sem,
):
    band, lane = lax.axis_index("band"), lax.axis_index("lon")
    me = band * lanes + lane
    devices = bands * lanes
    band_rows, points = factor_ref.shape
    rows, fields = grid_ref.shape[0], grid_ref.shape[1]
    own_fields, parts, latitudes, slot_count = coefficients.shape
    half = pair_band_ref.shape[-1]
    waves = 2 * half
    padded = wave_column.shape[0]
    width = 2 * padded
    cycle_points = lanes * points
    chunks = cycle_points // CHUNK
    entry = parts * own_fields
    entries = devices * rows
    chunk_rows = rows * entry
    stacked = chunk_rows * lanes
    groups = entries // GROUP
    group_devices = GROUP // rows
    unroll = devices <= 32

    def peer(k):
        flat = lax.rem(me + k, devices)
        return flat, {"band": flat // lanes, "lon": lax.rem(flat, lanes)}

    def block_of(index):
        return pl.ds(pl.multiple_of(index * points, LANES), points)

    def send_chunks(source, target, sent, received, far_first):
        def send(k, carry):
            flat, device = peer(devices - k if far_first else k)
            pltpu.make_async_remote_copy(
                src_ref=source.at[flat],
                dst_ref=target.at[me],
                send_sem=sent,
                recv_sem=received,
                device_id=device,
                device_id_type=MESH,
            ).start()
            return carry

        lax.fori_loop(1, devices, send, 0, unroll=unroll)
        target[me] = source[me]

    def wait_chunks(source, target, sent, received):
        pltpu.make_async_remote_copy(
            src_ref=source.at[pl.ds(0, devices - 1)],
            dst_ref=target.at[pl.ds(0, devices - 1)],
            send_sem=sent,
            recv_sem=received,
            device_id={"band": band, "lon": lane},
            device_id_type=MESH,
        ).wait()

    def factor_copy(j):
        return pltpu.make_async_remote_copy(
            src_ref=factor_ref,
            dst_ref=cycles.at[:, block_of(lane)],
            send_sem=factor_send_sem.at[j],
            recv_sem=factor_recv_sem.at[j],
            device_id={"lon": lax.rem(lane + j, lanes)},
            device_id_type=MESH,
        )

    def grid_copy(i, j):
        other = lax.rem(lane + j, lanes)
        return pltpu.make_async_remote_copy(
            src_ref=grid_ref.at[i, :, block_of(other)],
            dst_ref=blocks.at[lane, i],
            send_sem=grid_send_sem.at[i, j],
            recv_sem=grid_recv_sem.at[i, j],
            device_id={"lon": other},
            device_id_type=MESH,
        )

    barrier = pltpu.get_barrier_semaphore()

    def signal(k, carry):
        pl.semaphore_signal(barrier, inc=1, device_id=peer(k)[1], device_id_type=MESH)
        return carry

    inputs = [
        pltpu.make_async_copy(source, target, input_sem.at[index])
        for index, (source, target) in enumerate(
            (
                (latitude_hbm, latitude_ref),
                (coefficients_hbm, coefficients),
                (pair_band_hbm, pair_band_ref),
                (cycle_hbm, cycle_ref),
                (factor_hbm, factor_ref),
                (order_hbm, order_ref),
            )
        )
    ]
    lax.fori_loop(1, devices, signal, 0, unroll=unroll)
    for copy in inputs:
        copy.start()

    size = latitudes * entry
    part_row = lax.broadcasted_iota(jnp.int32, (entry, size), 0)
    offset = (lax.rem(part_row, own_fields) * parts + part_row // own_fields) * latitudes
    latitude_of = lax.broadcasted_iota(jnp.int32, (entry, size), 1) - offset

    def fill_pick(group):
        def one(pair, carry):
            pieces = []
            for side in range(2):
                number = group * GROUP + pair * 2 + side
                device, i = number // rows, lax.rem(number, rows)
                local = lax.rem(device, lanes) * rows + i
                row = (device // lanes) * band_rows + jnp.minimum(local, band_rows - 1)
                held = jnp.where(local < band_rows, latitude_ref[row], -(1 << 20))
                pieces.append(jnp.where(latitude_of == held, 1.0, 0.0))
            start = pl.multiple_of(pair * 2 * entry, 2 * entry)
            pick[pl.ds(start, 2 * entry), :] = jnp.concatenate(pieces, axis=0).astype(jnp.bfloat16)
            return carry

        lax.fori_loop(0, GROUP // 2, one, 0, unroll=4)

    def devices_of(group):
        return pl.ds(group * group_devices, group_devices)

    leaving[...] = jnp.zeros_like(leaving)
    inputs[0].wait()

    def gather(group, carry):
        fill_pick(group)
        if groups > 1:
            inputs_ready = coefficients[...]
        else:
            inputs[1].wait()
            inputs_ready = coefficients[...]
        picked = jnp.dot(
            pick[...], inputs_ready.reshape(size, slot_count), preferred_element_type=jnp.float32
        )
        picked = picked.reshape(group_devices, chunk_rows, slot_count).astype(jnp.bfloat16)
        leaving[devices_of(group), :, 0:slot_count] = picked
        return carry

    if groups > 1:
        inputs[1].wait()
        lax.fori_loop(0, groups, gather, 0)
    else:
        gather(0, 0)

    inputs[2].wait()
    pair_band = pair_band_ref[...].reshape(1, half)
    source = lax.broadcasted_iota(jnp.int32, (half, half), 0)
    target = lax.broadcasted_iota(jnp.int32, (half, half), 1)
    earlier = jnp.where(source < target, 1.0, 0.0).astype(jnp.bfloat16)
    padded_bands = -(-bands // 16) * 16
    owner = lax.broadcasted_iota(jnp.int32, (padded_bands, half), 0) == pair_band
    counts = jnp.dot(
        jnp.where(owner, 1.0, 0.0).astype(jnp.bfloat16), earlier, preferred_element_type=jnp.float32
    )
    place = jnp.sum(jnp.where(owner, counts, 0.0), axis=0, keepdims=True)
    slot_of_pair = pair_band * slot_count + place.astype(jnp.int32)
    slot = lax.broadcasted_iota(jnp.int32, (padded, half), 0)
    hot = jnp.where(slot == slot_of_pair, 1.0, 0.0).astype(jnp.bfloat16)
    number = lax.broadcasted_iota(jnp.int32, (half, 2 * LANES), 0) + 1
    upper = lax.broadcasted_iota(jnp.int32, (half, 2 * LANES), 1) < LANES
    digits = jnp.where(upper, number // 8, lax.rem(number, 8)).astype(jnp.float32)
    found = jnp.dot(hot, digits.astype(jnp.bfloat16), preferred_element_type=jnp.float32)
    wave_column[...] = found[:, :LANES] * 8.0 + found[:, LANES:]
    number = lax.broadcasted_iota(jnp.int32, (16, half), 1) + 1
    upper = lax.broadcasted_iota(jnp.int32, (16, half), 0) < 8
    digits = jnp.where(upper, number // 8, lax.rem(number, 8)).astype(jnp.float32)
    found = lax.dot_general(
        digits.astype(jnp.bfloat16),
        hot,
        (((1,), (1,)), ((), ())),
        preferred_element_type=jnp.float32,
    )
    ordinal = found[0:8] * 8.0 + found[8:16]
    wave_row = jnp.concatenate([ordinal - 1.0, waves - ordinal], axis=1)
    held_row = jnp.concatenate([ordinal, ordinal], axis=1) > 0.0

    inputs[3].wait()

    def length_of(i):
        row = jnp.minimum(lane * rows + i, band_rows - 1)
        n = cycle_ref[latitude_ref[band * band_rows + row]]
        length = jnp.full((1, 1), n, jnp.int32).astype(jnp.float32)
        return row, n, length, 1.0 / length

    def prepare_steps(i):
        row, n, length, inverse = length_of(i)
        step_ref[i, 0], step_ref[i, 1] = cos_sin(wave_row * float(CHUNK), length, inverse)
        step_ref[i, 2], step_ref[i, 3] = cos_sin(wave_row * float(2 * CHUNK), length, inverse)
        kept = jnp.where(held_row & (2.0 * wave_row < length), 1.0, 0.0)
        weight_ref[i] = kept

    def prepare_table(i):
        row, n, length, inverse = length_of(i)

        def block(step, carry):
            start = pl.multiple_of(step * 16, 16)
            ordinal = wave_column[pl.ds(start, 16), :]
            for member in range(2):
                wave = ordinal - 1.0 if member == 0 else waves - ordinal
                for side in range(CHUNK // LANES):
                    place = lax.broadcasted_iota(jnp.int32, (16, LANES), 1) + side * LANES
                    cosine, sine = cos_sin(wave * place.astype(jnp.float32), length, inverse)
                    at = pl.ds(member * padded + start, 16)
                    columns = slice(side * LANES, (side + 1) * LANES)
                    table[i, at, columns] = cosine.astype(jnp.bfloat16)
                    at = pl.ds(width + member * padded + start, 16)
                    table[i, at, columns] = (-sine).astype(jnp.bfloat16)
            return carry

        lax.fori_loop(0, padded // 16, block, 0)

    prepare_steps(0)
    prepare_table(0)
    inputs[4].wait()
    inputs[5].wait()

    pl.semaphore_wait(barrier, devices - 1)
    send_chunks(leaving, arrived, send_sem, recv_sem, True)
    for j in range(1, lanes):
        factor_copy(j).start()
    cycles[:, block_of(lane)] = factor_ref[...]

    for i in range(1, rows):
        prepare_steps(i)
        prepare_table(i)
    for j in range(1, lanes):
        factor_copy(j).wait()
    for i in range(rows):
        chosen = lax.broadcasted_iota(jnp.int32, (band_rows, 1), 0) == length_of(i)[0]
        row_factor[i] = jnp.sum(
            jnp.where(chosen, cycles[...].astype(jnp.float32), 0.0), axis=0, keepdims=True
        )

    wait_chunks(leaving, arrived, send_sem, recv_sem)

    lane_index = lax.broadcasted_iota(jnp.int32, (stacked, LANES), 1)
    pieces = []
    for b in range(bands):
        piece = arrived[b * lanes : (b + 1) * lanes].astype(jnp.float32)
        pieces.append(piece.reshape(stacked, LANES).astype(jnp.bfloat16))
    by_part = jnp.dot(
        order_ref[...], jnp.concatenate(pieces, axis=1), preferred_element_type=jnp.float32
    )
    columns = [None] * (padded // LANES)
    for b in range(bands):
        first = b * slot_count
        turn = first % LANES
        piece = by_part[:, b * LANES : (b + 1) * LANES]
        piece = pltpu.roll(piece, turn, 1) if turn else piece
        for v in range(first // LANES, (first + slot_count - 1) // LANES + 1):
            begin = first - v * LANES
            if columns[v] is None:
                columns[v] = piece
            else:
                columns[v] = jnp.where(lane_index >= begin, piece, columns[v])
    columns = [jnp.zeros((stacked, LANES), jnp.float32) if c is None else c for c in columns]
    compact = jnp.concatenate(columns, axis=1)
    first_wave = jnp.where(wave_row == 0.0, 1.0, 2.0)

    def tall(value, count):
        return jnp.concatenate([value] * (count // 8), axis=0)

    def part_of(member, t, i):
        return ((member * 2 + t) * rows + i) * fields

    for i in range(rows):
        row, n, length, inverse = length_of(i)
        norm = lax.rsqrt(length)
        live = tall(weight_ref[i] > 0.0, fields)
        scale = tall(first_wave, fields)
        state = []
        for t in range(2):
            held = jnp.concatenate(
                [compact[part_of(m, t, i) : part_of(m, t, i) + fields] for m in range(2)], axis=1
            )
            state.append(jnp.where(live, held * scale, 0.0))
        real, imag = state
        cosine, sine = tall(step_ref[i, 0], fields), tall(step_ref[i, 1], fields)
        real, imag = (
            jnp.concatenate([real, real * cosine - imag * sine], axis=0),
            jnp.concatenate([imag, real * sine + imag * cosine], axis=0),
        )
        cosine, sine = tall(step_ref[i, 2], 2 * fields), tall(step_ref[i, 3], 2 * fields)
        for h in range(chunks // 2):
            at = slice(2 * h * fields, 2 * (h + 1) * fields)
            lhs[i, at, 0:width] = real.astype(jnp.bfloat16)
            lhs[i, at, width : 2 * width] = imag.astype(jnp.bfloat16)
            if h < chunks // 2 - 1:
                real, imag = real * cosine - imag * sine, real * sine + imag * cosine

    for i in range(rows):
        row, n, length, inverse = length_of(i)
        norm = lax.rsqrt(length)
        found = jnp.dot(lhs[i], table[i], preferred_element_type=jnp.float32)
        for h in range(0, chunks, 2):
            pair = []
            for g in (h, h + 1):
                at = g * CHUNK + lax.broadcasted_iota(jnp.int32, (1, CHUNK), 1)
                value = found[g * fields : (g + 1) * fields]
                value = jnp.where(at < n, value * norm, 0.0).astype(jnp.bfloat16)
                grid_ref[i, :, g * CHUNK : (g + 1) * CHUNK] = value
                factor = row_factor[i, :, g * CHUNK : (g + 1) * CHUNK]
                pair.append(factor * value.astype(jnp.float32))
            product_ref[i, h * fields : (h + 2) * fields, :] = jnp.concatenate(
                pair, axis=0
            ).astype(jnp.bfloat16)
        for j in range(1, lanes):
            grid_copy(i, j).start()
        blocks[lane, i] = grid_ref[i, :, block_of(lane)]

    for i in range(rows):
        row, n, length, inverse = length_of(i)
        norm = lax.rsqrt(length)
        left = product_ref[i]
        for c in range(width // CHUNK):
            columns = slice(c * CHUNK, (c + 1) * CHUNK)
            parts_found = []
            for t in range(2):
                right = table[i, t * width + c * CHUNK : t * width + (c + 1) * CHUNK, :]
                parts_found.append(
                    lax.dot_general(
                        left, right, (((1,), (1,)), ((), ())), preferred_element_type=jnp.float32
                    )
                )
            cosine = tall(step_ref[i, 0, :, columns], fields)
            sine = tall(step_ref[i, 1, :, columns], fields)
            last = slice((chunks - 1) * fields, chunks * fields)
            real, imag = parts_found[0][last], parts_found[1][last]
            for h in range(chunks - 2, -1, -1):
                at = slice(h * fields, (h + 1) * fields)
                real, imag = (
                    real * cosine + imag * sine + parts_found[0][at],
                    imag * cosine - real * sine + parts_found[1][at],
                )
            scale = tall(weight_ref[i, :, columns], fields) * norm
            for t, value in ((0, real), (1, imag)):
                at = pl.ds((t * rows + i) * fields, fields)
                finished[at, columns] = value * scale

    spread = []
    for b in range(bands):
        first = b * slot_count
        turn = first % LANES
        v = first // LANES
        members = []
        for member in range(2):
            base = member * padded + v * LANES
            piece = finished[:, base : base + LANES]
            piece = pltpu.roll(piece, LANES - turn, 1) if turn else piece
            if turn + slot_count > LANES:
                after = pltpu.roll(finished[:, base + LANES : base + 2 * LANES], LANES - turn, 1)
                piece = jnp.where(lane_index[: piece.shape[0]] < LANES - turn, piece, after)
            members.append(piece)
        spread.append(jnp.concatenate(members, axis=0).astype(jnp.bfloat16))
    by_lane = lax.dot_general(
        order_ref[...],
        jnp.concatenate(spread, axis=1),
        (((0,), (0,)), ((), ())),
        preferred_element_type=jnp.float32,
    )
    for b in range(bands):
        piece = by_lane[:, b * LANES : (b + 1) * LANES].reshape(lanes, chunk_rows, LANES)
        result[b * lanes : (b + 1) * lanes] = piece.astype(jnp.bfloat16)

    send_chunks(result, returned, back_send_sem, back_recv_sem, False)
    for i in range(rows):
        for j in range(1, lanes):
            grid_copy(i, j).wait()
    wait_chunks(result, returned, back_send_sem, back_recv_sem)

    def place_group(group):
        held = returned[devices_of(group)].astype(jnp.float32)
        held = held.reshape(GROUP * entry, LANES).astype(jnp.bfloat16)
        return lax.dot_general(
            pick[...], held, (((0,), (0,)), ((), ())), preferred_element_type=jnp.float32
        )

    if groups == 1:
        placed = place_group(0)
    else:

        def add(group, total):
            fill_pick(group)
            return total + place_group(group)

        placed = lax.fori_loop(0, groups, add, jnp.zeros((size, LANES), jnp.float32))
    placed = placed[:, :slot_count].reshape(own_fields, parts, latitudes, slot_count)
    tendencies[...] = placed.astype(jnp.bfloat16)


def round_trip(coefficients, cycle_length, row_latitude, pair_band, factor, order, bands, lanes):
    devices = bands * lanes
    own_fields, parts, latitudes, slot_count = coefficients.shape
    fields = own_fields * lanes
    band_rows, points = factor.shape
    rows = -(-band_rows // lanes)
    entry = parts * own_fields
    padded = -(-bands * slot_count // LANES) * LANES
    width = 2 * padded
    chunks = lanes * points // CHUNK
    exchange = (devices, rows * entry, LANES)
    bf16, f32 = jnp.bfloat16, jnp.float32
    hbm = pl.BlockSpec(memory_space=pltpu.MemorySpace.HBM)
    return pl.pallas_call(
        functools.partial(round_kernel, bands, lanes),
        in_specs=[hbm] * 6,
        out_specs=[pl.BlockSpec(memory_space=pltpu.VMEM)] * 2,
        scratch_shapes=[
            pltpu.VMEM(coefficients.shape, bf16),
            pltpu.SMEM(cycle_length.shape, jnp.int32),
            pltpu.SMEM(row_latitude.shape, jnp.int32),
            pltpu.VMEM(pair_band.shape, jnp.int32),
            pltpu.VMEM(factor.shape, bf16),
            pltpu.VMEM(order.shape, bf16),
            pltpu.VMEM((GROUP * entry, latitudes * entry), bf16),
            pltpu.VMEM(exchange, bf16),
            pltpu.VMEM(exchange, bf16),
            pltpu.VMEM(exchange, bf16),
            pltpu.VMEM(exchange, bf16),
            pltpu.VMEM((band_rows, lanes * points), bf16),
            pltpu.VMEM((rows, fields, lanes * points), bf16),
            pltpu.VMEM((rows, 2 * width, CHUNK), bf16),
            pltpu.VMEM((rows, chunks * fields, 2 * width), bf16),
            pltpu.VMEM((rows, chunks * fields, CHUNK), bf16),
            pltpu.VMEM((rows, 1, lanes * points), f32),
            pltpu.VMEM((padded, LANES), f32),
            pltpu.VMEM((rows, 4, 8, width), f32),
            pltpu.VMEM((rows, 8, width), f32),
            pltpu.VMEM((2 * rows * fields, width), f32),
        ]
        + [pltpu.SemaphoreType.DMA((6,))]
        + [pltpu.SemaphoreType.DMA] * 4
        + [pltpu.SemaphoreType.DMA((lanes,))] * 2
        + [pltpu.SemaphoreType.DMA((rows, lanes))] * 2,
        out_shape=[
            jax.ShapeDtypeStruct((lanes, rows, fields, points), bf16),
            jax.ShapeDtypeStruct(coefficients.shape, bf16),
        ],
        compiler_params=pltpu.CompilerParams(
            collective_id=0, has_side_effects=True, vmem_limit_bytes=40 << 20
        ),
    )(
        *[
            pltpu.with_memory_space_constraint(array, pltpu.MemorySpace.HBM)
            for array in (coefficients, cycle_length, row_latitude, pair_band, factor, order)
        ]
    )


def on_device(coefficients, cycle_length, row_latitude, pair_band, gridpoint_factor):
    bands, lanes = lax.axis_size("band"), lax.axis_size("lon")
    own_fields, slot_count, parts, latitudes = coefficients.shape
    band_rows, points = gridpoint_factor.shape
    fields = own_fields * lanes
    own_rows = -(-band_rows // lanes)
    stacked = lanes * own_rows * parts * own_fields
    places = np.arange(stacked).reshape(lanes, own_rows, parts, own_fields)
    places = places.transpose(2, 1, 0, 3).reshape(-1)
    order = jnp.asarray(places[:, None] == np.arange(stacked)[None, :], dtype=jnp.bfloat16)
    blocks, placed = round_trip(
        jnp.transpose(coefficients, (0, 2, 3, 1)),
        cycle_length,
        row_latitude,
        pair_band,
        gridpoint_factor,
        order,
        bands,
        lanes,
    )
    grid_rows = blocks.reshape(lanes * own_rows, fields, points)[:band_rows]
    return (jnp.transpose(grid_rows, (1, 0, 2)), jnp.transpose(placed, (0, 3, 1, 2)))


def solution(mesh):
    return jax.shard_map(
        on_device,
        mesh=mesh,
        in_specs=(P("lon", "band", None, None), P(), P(), P(), P("band", "lon")),
        out_specs=(P(None, "band", "lon"), P("lon", "band", None, None)),
        check_vma=False,
    )
```

```python
import functools
import math

import jax
import jax.numpy as jnp
import numpy as np
from jax import lax
from jax.experimental import pallas as pl
from jax.experimental.pallas import tpu as pltpu
from jax.sharding import PartitionSpec as P

TWO_PI = 2.0 * math.pi
LANES = 128
CHUNK = 256
GROUP = 64
MESH = pl.DeviceIdType.MESH
LOGICAL = pl.DeviceIdType.LOGICAL


def cos_sin(product, length, inverse):
    turns = jnp.floor(product * inverse + 0.5)
    half = (product - turns * length) * (inverse * (0.5 * TWO_PI))
    square = half * half
    sine = jnp.full_like(half, -1.0 / math.factorial(11))
    for order in (9, 7, 5, 3, 1):
        sine = sine * square + (-1.0) ** (order // 2) / math.factorial(order)
    sine = sine * half
    cosine = jnp.full_like(half, 1.0 / math.factorial(12))
    for order in (10, 8, 6, 4, 2, 0):
        cosine = cosine * square + (-1.0) ** (order // 2) / math.factorial(order)
    return 1.0 - 2.0 * sine * sine, 2.0 * sine * cosine


def round_kernel(
    bands,
    lanes,
    coefficients_hbm,
    cycle_hbm,
    latitude_hbm,
    pair_band_hbm,
    factor_hbm,
    order_hbm,
    blocks,
    tendencies,
    coefficients,
    cycle_ref,
    latitude_ref,
    pair_band_ref,
    factor_ref,
    order_ref,
    pick,
    leaving,
    arrived,
    result,
    returned,
    cycles,
    grid_ref,
    table,
    lhs,
    product_ref,
    row_factor,
    wave_column,
    step_ref,
    weight_ref,
    finished,
    input_sem,
    send_sem,
    recv_sem,
    back_send_sem,
    back_recv_sem,
    factor_send_sem,
    factor_recv_sem,
    grid_send_sem,
    grid_recv_sem,
):
    band, lane = lax.axis_index("band"), lax.axis_index("lon")
    me = band * lanes + lane
    devices = bands * lanes
    band_rows, points = factor_ref.shape
    rows, fields = grid_ref.shape[0], grid_ref.shape[1]
    own_fields, parts, latitudes, slot_count = coefficients.shape
    half = pair_band_ref.shape[-1]
    waves = 2 * half
    padded = wave_column.shape[0]
    width = 2 * padded
    cycle_points = lanes * points
    chunks = cycle_points // CHUNK
    entry = parts * own_fields
    entries = devices * rows
    stacked = entry * lanes
    groups = entries // GROUP
    every = slice(0, rows)
    unroll = devices <= 32

    plane = 2 * lanes
    planes = devices // plane
    own_plane = lax.div(band, 2)
    own_place = me - own_plane * plane
    upper_half = own_plane >= planes - planes // 2

    def for_peers(act, first_planes):
        def place_at(turn):
            place = own_place + turn
            return jnp.where(place >= plane, place - plane, place)

        def facing(shift):
            level = own_plane + shift
            level = jnp.where(level >= planes, level - planes, level)
            act(level * plane + own_place)

        def others(step, turn):
            level = jnp.where(first_planes, step, planes - 1 - step)
            act(level * plane + place_at(turn))

        if unroll:
            for shift in range(1, planes):
                facing(shift)
            for step in range(planes):
                for turn in range(1, plane):
                    others(step, turn)
        else:
            lax.fori_loop(1, planes, lambda shift, carry: (facing(shift), carry)[1], 0)

            def one(step, carry):
                return lax.fori_loop(1, plane, lambda turn, c: (others(step, turn), c)[1], carry)

            lax.fori_loop(0, planes, one, 0)

    def block_of(index):
        return pl.ds(pl.multiple_of(index * points, LANES), points)

    def send_chunks(source, target, sent, received, row, first_planes):
        def send(flat):
            pltpu.make_async_remote_copy(
                src_ref=source.at[row, flat],
                dst_ref=target.at[row, me],
                send_sem=sent,
                recv_sem=received,
                device_id=flat,
                device_id_type=LOGICAL,
            ).start()

        for_peers(send, first_planes)
        target[row, me] = source[row, me]

    def wait_chunks(source, target, sent, received, row):
        pltpu.make_async_remote_copy(
            src_ref=source.at[row, pl.ds(0, devices - 1)],
            dst_ref=target.at[row, pl.ds(0, devices - 1)],
            send_sem=sent,
            recv_sem=received,
            device_id={"band": band, "lon": lane},
            device_id_type=MESH,
        ).wait()

    def factor_copy(j):
        return pltpu.make_async_remote_copy(
            src_ref=factor_ref,
            dst_ref=cycles.at[:, block_of(lane)],
            send_sem=factor_send_sem.at[j],
            recv_sem=factor_recv_sem.at[j],
            device_id={"lon": lax.rem(lane + j, lanes)},
            device_id_type=MESH,
        )

    def grid_copy(i, j):
        other = lax.rem(lane + j, lanes)
        return pltpu.make_async_remote_copy(
            src_ref=grid_ref.at[i, :, block_of(other)],
            dst_ref=blocks.at[lane, i],
            send_sem=grid_send_sem.at[i, j],
            recv_sem=grid_recv_sem.at[i, j],
            device_id={"lon": other},
            device_id_type=MESH,
        )

    barrier = pltpu.get_barrier_semaphore()

    def signal(flat):
        pl.semaphore_signal(barrier, inc=1, device_id=flat, device_id_type=LOGICAL)

    inputs = [
        pltpu.make_async_copy(source, target, input_sem.at[index])
        for index, (source, target) in enumerate(
            (
                (latitude_hbm, latitude_ref),
                (coefficients_hbm, coefficients),
                (pair_band_hbm, pair_band_ref),
                (cycle_hbm, cycle_ref),
                (factor_hbm, factor_ref),
                (order_hbm, order_ref),
            )
        )
    ]
    for_peers(signal, upper_half)
    for copy in inputs:
        copy.start()

    size = latitudes * entry
    part_row = lax.broadcasted_iota(jnp.int32, (entry, size), 0)
    offset = (lax.rem(part_row, own_fields) * parts + part_row // own_fields) * latitudes
    latitude_of = lax.broadcasted_iota(jnp.int32, (entry, size), 1) - offset

    def fill_pick(group):
        def one(pair, carry):
            pieces = []
            for side in range(2):
                number = group * GROUP + pair * 2 + side
                if band_rows == lanes * rows:
                    i, device = lax.div(number, devices), lax.rem(number, devices)
                    held = latitude_ref[device * rows + i]
                else:
                    i, device = lax.div(number, devices), lax.rem(number, devices)
                    local = lax.rem(device, lanes) * rows + i
                    row = (device // lanes) * band_rows + jnp.minimum(local, band_rows - 1)
                    held = jnp.where(local < band_rows, latitude_ref[row], -(1 << 20))
                pieces.append(jnp.where(latitude_of == held, 1.0, 0.0))
            start = pl.multiple_of(pair * 2 * entry, 2 * entry)
            pick[pl.ds(start, 2 * entry), :] = jnp.concatenate(pieces, axis=0).astype(jnp.bfloat16)
            return carry

        lax.fori_loop(0, GROUP // 2, one, 0, unroll=4)

    leaving[...] = jnp.zeros_like(leaving)
    inputs[0].wait()

    def gather(group, carry):
        fill_pick(group)
        if groups > 1:
            inputs_ready = coefficients[...]
        else:
            inputs[1].wait()
            inputs_ready = coefficients[...]
        picked = jnp.dot(
            pick[...], inputs_ready.reshape(size, slot_count), preferred_element_type=jnp.float32
        )
        if groups > 1:
            picked = picked.reshape(GROUP, entry, slot_count).astype(jnp.bfloat16)
            leaving[0, pl.ds(group * GROUP, GROUP), :, 0:slot_count] = picked
        else:
            picked = picked.reshape(rows, devices, entry, slot_count).astype(jnp.bfloat16)
            leaving[:, :, :, 0:slot_count] = picked
        return carry

    if groups > 1:
        inputs[1].wait()
        lax.fori_loop(0, groups, gather, 0)
    else:
        gather(0, 0)

    inputs[2].wait()
    pair_band = pair_band_ref[...].reshape(1, half)
    source = lax.broadcasted_iota(jnp.int32, (half, half), 0)
    target = lax.broadcasted_iota(jnp.int32, (half, half), 1)
    earlier = jnp.where(source < target, 1.0, 0.0).astype(jnp.bfloat16)
    padded_bands = -(-bands // 16) * 16
    owner = lax.broadcasted_iota(jnp.int32, (padded_bands, half), 0) == pair_band
    counts = jnp.dot(
        jnp.where(owner, 1.0, 0.0).astype(jnp.bfloat16), earlier, preferred_element_type=jnp.float32
    )
    place = jnp.sum(jnp.where(owner, counts, 0.0), axis=0, keepdims=True)
    slot_of_pair = pair_band * slot_count + place.astype(jnp.int32)
    slot = lax.broadcasted_iota(jnp.int32, (padded, half), 0)
    hot = jnp.where(slot == slot_of_pair, 1.0, 0.0).astype(jnp.bfloat16)
    number = lax.broadcasted_iota(jnp.int32, (half, 2 * LANES), 0) + 1
    upper = lax.broadcasted_iota(jnp.int32, (half, 2 * LANES), 1) < LANES
    digits = jnp.where(upper, number // 8, lax.rem(number, 8)).astype(jnp.float32)
    found = jnp.dot(hot, digits.astype(jnp.bfloat16), preferred_element_type=jnp.float32)
    wave_column[...] = found[:, :LANES] * 8.0 + found[:, LANES:]
    number = lax.broadcasted_iota(jnp.int32, (16, half), 1) + 1
    upper = lax.broadcasted_iota(jnp.int32, (16, half), 0) < 8
    digits = jnp.where(upper, number // 8, lax.rem(number, 8)).astype(jnp.float32)
    found = lax.dot_general(
        digits.astype(jnp.bfloat16),
        hot,
        (((1,), (1,)), ((), ())),
        preferred_element_type=jnp.float32,
    )
    ordinal = found[0:8] * 8.0 + found[8:16]
    wave_row = jnp.concatenate([ordinal - 1.0, waves - ordinal], axis=1)
    held_row = jnp.concatenate([ordinal, ordinal], axis=1) > 0.0

    inputs[3].wait()

    def tall(value, count):
        return jnp.concatenate([value] * (count // 8), axis=0)

    def length_of(i):
        row = jnp.minimum(lane * rows + i, band_rows - 1)
        n = cycle_ref[latitude_ref[band * band_rows + row]]
        length = jnp.full((1, 1), n, jnp.int32).astype(jnp.float32)
        return row, n, length, 1.0 / length

    def prepare_steps(i):
        row, n, length, inverse = length_of(i)
        step_ref[i, 0], step_ref[i, 1] = cos_sin(wave_row * float(CHUNK), length, inverse)
        step_ref[i, 2], step_ref[i, 3] = cos_sin(wave_row * float(2 * CHUNK), length, inverse)
        kept = jnp.where(held_row & (2.0 * wave_row < length), 1.0, 0.0)
        weight_ref[i] = kept

    def prepare_table(i, begin, end):
        row, n, length, inverse = length_of(i)

        places = lax.broadcasted_iota(jnp.int32, (8, CHUNK), 1).astype(jnp.float32)
        last_cosine, last_sine = cos_sin(places * float(waves - 1), length, inverse)

        def block(step, carry):
            start = pl.multiple_of(step * 16, 16)
            ordinal = wave_column[pl.ds(start, 16), :]
            for side in range(CHUNK // LANES):
                columns = slice(side * LANES, (side + 1) * LANES)
                place = lax.broadcasted_iota(jnp.int32, (16, LANES), 1) + side * LANES
                product = (ordinal - 1.0) * place.astype(jnp.float32)
                cosine, sine = cos_sin(product, length, inverse)
                top_cosine = tall(last_cosine[:, columns], 16)
                top_sine = tall(last_sine[:, columns], 16)
                pairs = (
                    (cosine, sine),
                    (
                        top_cosine * cosine + top_sine * sine,
                        top_sine * cosine - top_cosine * sine,
                    ),
                )
                for member, (cosine, sine) in enumerate(pairs):
                    at = pl.ds(member * padded + start, 16)
                    table[i, at, columns] = cosine.astype(jnp.bfloat16)
                    at = pl.ds(width + member * padded + start, 16)
                    table[i, at, columns] = (-sine).astype(jnp.bfloat16)
            return carry

        lax.fori_loop(begin, end, block, 0)

    blocks_all = padded // 16
    quarter = lax.div(own_plane * 4, planes)
    early = [jnp.where(quarter == 3, blocks_all // 2, blocks_all)]
    early += [jnp.where(quarter == 0, blocks_all, 0)] * (rows - 1)
    for i in range(rows):
        prepare_table(i, 0, early[i])
    inputs[4].wait()
    inputs[5].wait()

    pl.semaphore_wait(barrier, devices - 1)
    send_chunks(leaving, arrived, send_sem, recv_sem, every, upper_half)
    for j in range(1, lanes):
        factor_copy(j).start()
    cycles[:, block_of(lane)] = factor_ref[...]

    for i in range(rows):
        prepare_steps(i)
        prepare_table(i, early[i], blocks_all)
    for j in range(1, lanes):
        factor_copy(j).wait()
    for i in range(rows):
        chosen = lax.broadcasted_iota(jnp.int32, (band_rows, 1), 0) == length_of(i)[0]
        row_factor[i] = jnp.sum(
            jnp.where(chosen, cycles[...].astype(jnp.float32), 0.0), axis=0, keepdims=True
        )

    wait_chunks(leaving, arrived, send_sem, recv_sem, every)

    lane_index = lax.broadcasted_iota(jnp.int32, (stacked, LANES), 1)
    def compact_of(i):
        pieces = []
        for b in range(bands):
            piece = arrived[i, b * lanes : (b + 1) * lanes].astype(jnp.float32)
            pieces.append(piece.reshape(stacked, LANES).astype(jnp.bfloat16))
        by_part = jnp.dot(
            order_ref[...], jnp.concatenate(pieces, axis=1), preferred_element_type=jnp.float32
        )
        columns = [jnp.zeros((stacked, LANES), jnp.float32)] * (padded // LANES)
        for b in range(bands):
            first = b * slot_count
            turn = first % LANES
            piece = by_part[:, b * LANES : (b + 1) * LANES]
            piece = pltpu.roll(piece, turn, 1) if turn else piece
            for v in range(first // LANES, (first + slot_count - 1) // LANES + 1):
                begin = first - v * LANES
                if begin <= 0:
                    columns[v] = piece
                else:
                    columns[v] = jnp.where(lane_index >= begin, piece, columns[v])
        return jnp.concatenate(columns, axis=1)

    first_wave = jnp.where(wave_row == 0.0, 1.0, 2.0)

    def part_of(member, t):
        return (member * 2 + t) * fields

    for i in range(rows):
        row, n, length, inverse = length_of(i)
        norm = lax.rsqrt(length)
        live = tall(weight_ref[i] > 0.0, fields)
        scale = tall(first_wave, fields)
        state = []
        compact = compact_of(i)
        for t in range(2):
            held = jnp.concatenate(
                [compact[part_of(m, t) : part_of(m, t) + fields] for m in range(2)], axis=1
            )
            state.append(jnp.where(live, held * scale, 0.0))
        real, imag = state
        cosine, sine = tall(step_ref[i, 0], fields), tall(step_ref[i, 1], fields)
        real, imag = (
            jnp.concatenate([real, real * cosine - imag * sine], axis=0),
            jnp.concatenate([imag, real * sine + imag * cosine], axis=0),
        )
        cosine, sine = tall(step_ref[i, 2], 2 * fields), tall(step_ref[i, 3], 2 * fields)
        for h in range(chunks // 2):
            at = slice(2 * h * fields, 2 * (h + 1) * fields)
            lhs[i, at, 0:width] = real.astype(jnp.bfloat16)
            lhs[i, at, width : 2 * width] = imag.astype(jnp.bfloat16)
            if h < chunks // 2 - 1:
                real, imag = real * cosine - imag * sine, real * sine + imag * cosine

    for i in range(rows):
        row, n, length, inverse = length_of(i)
        norm = lax.rsqrt(length)
        found = jnp.dot(lhs[i], table[i], preferred_element_type=jnp.float32)
        for h in range(0, chunks, 2):
            pair = []
            for g in (h, h + 1):
                at = g * CHUNK + lax.broadcasted_iota(jnp.int32, (1, CHUNK), 1)
                value = found[g * fields : (g + 1) * fields]
                value = jnp.where(at < n, value * norm, 0.0).astype(jnp.bfloat16)
                grid_ref[i, :, g * CHUNK : (g + 1) * CHUNK] = value
                factor = row_factor[i, :, g * CHUNK : (g + 1) * CHUNK]
                pair.append(factor * value.astype(jnp.float32))
            product_ref[i, h * fields : (h + 2) * fields, :] = jnp.concatenate(
                pair, axis=0
            ).astype(jnp.bfloat16)
        for j in range(1, lanes):
            grid_copy(i, j).start()
        blocks[lane, i] = grid_ref[i, :, block_of(lane)]

    def finish_row(i):
        spread = []
        for b in range(bands):
            first = b * slot_count
            turn = first % LANES
            v = first // LANES
            members = []
            for member in range(2):
                base = member * padded + v * LANES
                piece = finished[i, :, base : base + LANES]
                piece = pltpu.roll(piece, LANES - turn, 1) if turn else piece
                if turn + slot_count > LANES:
                    after = finished[i, :, base + LANES : base + 2 * LANES]
                    after = pltpu.roll(after, LANES - turn, 1)
                    piece = jnp.where(lane_index[: 2 * fields] < LANES - turn, piece, after)
                members.append(piece)
            spread.append(jnp.concatenate(members, axis=0).astype(jnp.bfloat16))
        by_lane = lax.dot_general(
            order_ref[...],
            jnp.concatenate(spread, axis=1),
            (((0,), (0,)), ((), ())),
            preferred_element_type=jnp.float32,
        )
        for b in range(bands):
            piece = by_lane[:, b * LANES : (b + 1) * LANES].reshape(lanes, entry, LANES)
            result[i, b * lanes : (b + 1) * lanes] = piece.astype(jnp.bfloat16)
        send_chunks(result, returned, back_send_sem.at[i], back_recv_sem.at[i], i, True)

    for i in range(rows):
        row, n, length, inverse = length_of(i)
        norm = lax.rsqrt(length)
        left = product_ref[i]
        for c in range(width // CHUNK):
            columns = slice(c * CHUNK, (c + 1) * CHUNK)
            parts_found = []
            for t in range(2):
                right = table[i, t * width + c * CHUNK : t * width + (c + 1) * CHUNK, :]
                parts_found.append(
                    lax.dot_general(
                        left, right, (((1,), (1,)), ((), ())), preferred_element_type=jnp.float32
                    )
                )
            cosine = tall(step_ref[i, 0, :, columns], fields)
            sine = tall(step_ref[i, 1, :, columns], fields)
            last = slice((chunks - 1) * fields, chunks * fields)
            real, imag = parts_found[0][last], parts_found[1][last]
            for h in range(chunks - 2, -1, -1):
                at = slice(h * fields, (h + 1) * fields)
                real, imag = (
                    real * cosine + imag * sine + parts_found[0][at],
                    imag * cosine - real * sine + parts_found[1][at],
                )
            scale = tall(weight_ref[i, :, columns], fields) * norm
            for t, value in ((0, real), (1, imag)):
                finished[i, t * fields : (t + 1) * fields, columns] = value * scale
        finish_row(i)

    for i in range(rows):
        for j in range(1, lanes):
            grid_copy(i, j).wait()
    for i in range(rows):
        wait_chunks(result, returned, back_send_sem.at[i], back_recv_sem.at[i], i)

    def place_group(group):
        if groups > 1:
            held = returned[0, pl.ds(group * GROUP, GROUP)].astype(jnp.float32)
        else:
            held = returned[...].astype(jnp.float32)
        held = held.reshape(GROUP * entry, LANES).astype(jnp.bfloat16)
        return lax.dot_general(
            pick[...], held, (((0,), (0,)), ((), ())), preferred_element_type=jnp.float32
        )

    if groups == 1:
        placed = place_group(0)
    else:

        def add(group, total):
            fill_pick(group)
            return total + place_group(group)

        placed = lax.fori_loop(0, groups, add, jnp.zeros((size, LANES), jnp.float32))
    placed = placed[:, :slot_count].reshape(own_fields, parts, latitudes, slot_count)
    tendencies[...] = placed.astype(jnp.bfloat16)


def round_trip(coefficients, cycle_length, row_latitude, pair_band, factor, order, bands, lanes):
    devices = bands * lanes
    own_fields, parts, latitudes, slot_count = coefficients.shape
    fields = own_fields * lanes
    band_rows, points = factor.shape
    rows = -(-band_rows // lanes)
    entry = parts * own_fields
    padded = -(-bands * slot_count // LANES) * LANES
    width = 2 * padded
    chunks = lanes * points // CHUNK
    exchange = (rows, devices, entry, LANES)
    bf16, f32 = jnp.bfloat16, jnp.float32
    hbm = pl.BlockSpec(memory_space=pltpu.MemorySpace.HBM)
    return pl.pallas_call(
        functools.partial(round_kernel, bands, lanes),
        in_specs=[hbm] * 6,
        out_specs=[pl.BlockSpec(memory_space=pltpu.VMEM)] * 2,
        scratch_shapes=[
            pltpu.VMEM(coefficients.shape, bf16),
            pltpu.SMEM(cycle_length.shape, jnp.int32),
            pltpu.SMEM(row_latitude.shape, jnp.int32),
            pltpu.VMEM(pair_band.shape, jnp.int32),
            pltpu.VMEM(factor.shape, bf16),
            pltpu.VMEM(order.shape, bf16),
            pltpu.VMEM((GROUP * entry, latitudes * entry), bf16),
            pltpu.VMEM(exchange, bf16),
            pltpu.VMEM(exchange, bf16),
            pltpu.VMEM(exchange, bf16),
            pltpu.VMEM(exchange, bf16),
            pltpu.VMEM((band_rows, lanes * points), bf16),
            pltpu.VMEM((rows, fields, lanes * points), bf16),
            pltpu.VMEM((rows, 2 * width, CHUNK), bf16),
            pltpu.VMEM((rows, chunks * fields, 2 * width), bf16),
            pltpu.VMEM((rows, chunks * fields, CHUNK), bf16),
            pltpu.VMEM((rows, 1, lanes * points), f32),
            pltpu.VMEM((padded, LANES), f32),
            pltpu.VMEM((rows, 4, 8, width), f32),
            pltpu.VMEM((rows, 8, width), f32),
            pltpu.VMEM((rows, 2 * fields, width), f32),
        ]
        + [pltpu.SemaphoreType.DMA((6,))]
        + [pltpu.SemaphoreType.DMA] * 2
        + [pltpu.SemaphoreType.DMA((rows,))] * 2
        + [pltpu.SemaphoreType.DMA((lanes,))] * 2
        + [pltpu.SemaphoreType.DMA((rows, lanes))] * 2,
        out_shape=[
            jax.ShapeDtypeStruct((lanes, rows, fields, points), bf16),
            jax.ShapeDtypeStruct(coefficients.shape, bf16),
        ],
        compiler_params=pltpu.CompilerParams(
            collective_id=0, has_side_effects=True, vmem_limit_bytes=40 << 20
        ),
    )(
        *[
            pltpu.with_memory_space_constraint(array, pltpu.MemorySpace.HBM)
            for array in (coefficients, cycle_length, row_latitude, pair_band, factor, order)
        ]
    )


def place_kernel(blocks, placed, grid_out, tendencies_out, grid_ref, sem):
    tendencies_copy = pltpu.make_async_copy(placed, tendencies_out, sem.at[0])
    tendencies_copy.start()
    lanes, rows, fields, points = blocks.shape
    held = blocks[...].astype(jnp.float32).reshape(lanes * rows, fields, points)
    grid_ref[...] = jnp.swapaxes(held, 0, 1).astype(jnp.bfloat16)
    grid_copy = pltpu.make_async_copy(grid_ref, grid_out, sem.at[1])
    grid_copy.start()
    tendencies_copy.wait()
    grid_copy.wait()


def place_outputs(blocks, placed):
    lanes, rows, fields, points = blocks.shape
    grid_shape = (fields, lanes * rows, points)
    return pl.pallas_call(
        place_kernel,
        in_specs=[pl.BlockSpec(memory_space=pltpu.VMEM)] * 2,
        out_specs=[pl.BlockSpec(memory_space=pl.ANY)] * 2,
        out_shape=[
            jax.ShapeDtypeStruct(grid_shape, jnp.bfloat16),
            jax.ShapeDtypeStruct(placed.shape, jnp.bfloat16),
        ],
        scratch_shapes=[pltpu.VMEM(grid_shape, jnp.bfloat16), pltpu.SemaphoreType.DMA((2,))],
        compiler_params=pltpu.CompilerParams(vmem_limit_bytes=16 << 20),
    )(blocks, placed)


def on_device(coefficients, cycle_length, row_latitude, pair_band, gridpoint_factor):
    bands, lanes = lax.axis_size("band"), lax.axis_size("lon")
    own_fields, slot_count, parts, latitudes = coefficients.shape
    band_rows, points = gridpoint_factor.shape
    fields = own_fields * lanes
    own_rows = -(-band_rows // lanes)
    stacked = lanes * parts * own_fields
    places = np.arange(stacked).reshape(lanes, parts, own_fields)
    places = places.transpose(1, 0, 2).reshape(-1)
    order = jnp.asarray(places[:, None] == np.arange(stacked)[None, :], dtype=jnp.bfloat16)
    blocks, placed = round_trip(
        jnp.transpose(coefficients, (0, 2, 3, 1)),
        cycle_length,
        row_latitude,
        pair_band,
        gridpoint_factor,
        order,
        bands,
        lanes,
    )
    if lanes * own_rows == band_rows and band_rows % 8 == 0 and fields % 8 == 0:
        grid, placed = place_outputs(blocks, placed)
        return (grid, jnp.transpose(placed, (0, 3, 1, 2)))
    grid_rows = blocks.reshape(lanes * own_rows, fields, points)[:band_rows]
    return (jnp.transpose(grid_rows, (1, 0, 2)), jnp.transpose(placed, (0, 3, 1, 2)))


def solution(mesh):
    return jax.shard_map(
        on_device,
        mesh=mesh,
        in_specs=(P("lon", "band", None, None), P(), P(), P(), P("band", "lon")),
        out_specs=(P(None, "band", "lon"), P("lon", "band", None, None)),
        check_vma=False,
    )
```

```python
import functools
import math

import jax
import jax.numpy as jnp
import numpy as np
from jax import lax
from jax.experimental import pallas as pl
from jax.experimental.pallas import tpu as pltpu
from jax.sharding import PartitionSpec as P

TWO_PI = 2.0 * math.pi
LANES = 128
CHUNK = 256
GROUP = 64
MESH = pl.DeviceIdType.MESH
LOGICAL = pl.DeviceIdType.LOGICAL


def cos_sin(product, length, inverse):
    turns = jnp.floor(product * inverse + 0.5)
    half = (product - turns * length) * (inverse * (0.5 * TWO_PI))
    square = half * half
    sine = jnp.full_like(half, -1.0 / math.factorial(11))
    for order in (9, 7, 5, 3, 1):
        sine = sine * square + (-1.0) ** (order // 2) / math.factorial(order)
    sine = sine * half
    cosine = jnp.full_like(half, 1.0 / math.factorial(12))
    for order in (10, 8, 6, 4, 2, 0):
        cosine = cosine * square + (-1.0) ** (order // 2) / math.factorial(order)
    return 1.0 - 2.0 * sine * sine, 2.0 * sine * cosine


def round_kernel(
    bands,
    lanes,
    coefficients_hbm,
    cycle_hbm,
    latitude_hbm,
    pair_band_hbm,
    factor_hbm,
    order_hbm,
    grid_out,
    tendencies,
    blocks,
    coefficients,
    cycle_ref,
    latitude_ref,
    pair_band_ref,
    factor_ref,
    order_ref,
    pick,
    leaving,
    arrived,
    result,
    returned,
    cycles,
    grid_ref,
    table,
    lhs,
    product_ref,
    row_factor,
    wave_column,
    step_ref,
    weight_ref,
    finished,
    input_sem,
    send_sem,
    recv_sem,
    back_send_sem,
    back_recv_sem,
    factor_send_sem,
    factor_recv_sem,
    grid_send_sem,
    grid_recv_sem,
):
    band, lane = lax.axis_index("band"), lax.axis_index("lon")
    me = band * lanes + lane
    devices = bands * lanes
    band_rows, points = factor_ref.shape
    rows, fields = grid_ref.shape[0], grid_ref.shape[1]
    own_fields, parts, latitudes, slot_count = coefficients.shape
    half = pair_band_ref.shape[-1]
    waves = 2 * half
    padded = wave_column.shape[0]
    width = 2 * padded
    cycle_points = lanes * points
    chunks = cycle_points // CHUNK
    entry = parts * own_fields
    entries = devices * rows
    stacked = entry * lanes
    groups = entries // GROUP
    every = slice(0, rows)
    main, rest = LANES // 2, LANES // 8
    packed = bands == 8 and entry == 8 and groups == 1 and main < slot_count <= main + rest
    wire = slice(0, 6) if packed else slice(0, entry)
    unroll = devices <= 32

    plane = 2 * lanes
    planes = devices // plane
    own_plane = lax.div(band, 2)
    own_place = me - own_plane * plane
    upper_half = own_plane >= planes - planes // 2

    def for_peers(act, first_planes):
        def place_at(turn):
            place = own_place + turn
            return jnp.where(place >= plane, place - plane, place)

        def facing(shift):
            level = own_plane + shift
            level = jnp.where(level >= planes, level - planes, level)
            act(level * plane + own_place)

        def others(step, turn):
            level = jnp.where(first_planes, step, planes - 1 - step)
            act(level * plane + place_at(turn))

        if unroll:
            for shift in range(1, planes):
                facing(shift)
            for step in range(planes):
                for turn in range(1, plane):
                    others(step, turn)
        else:
            lax.fori_loop(1, planes, lambda shift, carry: (facing(shift), carry)[1], 0)

            def one(step, carry):
                return lax.fori_loop(1, plane, lambda turn, c: (others(step, turn), c)[1], carry)

            lax.fori_loop(0, planes, one, 0)

    def block_of(index):
        return pl.ds(pl.multiple_of(index * points, LANES), points)

    def send_chunks(source, target, sent, received, row, first_planes):
        def send(flat):
            pltpu.make_async_remote_copy(
                src_ref=source.at[row, flat, wire],
                dst_ref=target.at[row, me, wire],
                send_sem=sent,
                recv_sem=received,
                device_id=flat,
                device_id_type=LOGICAL,
            ).start()

        for_peers(send, first_planes)
        target[row, me] = source[row, me]

    def wait_chunks(source, target, sent, received, row):
        pltpu.make_async_remote_copy(
            src_ref=source.at[row, pl.ds(0, devices - 1), wire],
            dst_ref=target.at[row, pl.ds(0, devices - 1), wire],
            send_sem=sent,
            recv_sem=received,
            device_id={"band": band, "lon": lane},
            device_id_type=MESH,
        ).wait()

    def factor_copy(j):
        return pltpu.make_async_remote_copy(
            src_ref=factor_ref,
            dst_ref=cycles.at[:, block_of(lane)],
            send_sem=factor_send_sem.at[j],
            recv_sem=factor_recv_sem.at[j],
            device_id={"lon": lax.rem(lane + j, lanes)},
            device_id_type=MESH,
        )

    def grid_copy(i, j):
        other = lax.rem(lane + j, lanes)
        return pltpu.make_async_remote_copy(
            src_ref=grid_ref.at[i, :, block_of(other)],
            dst_ref=blocks.at[lane, i],
            send_sem=grid_send_sem.at[i, j],
            recv_sem=grid_recv_sem.at[i, j],
            device_id={"lon": other},
            device_id_type=MESH,
        )

    barrier = pltpu.get_barrier_semaphore()

    def signal(flat):
        pl.semaphore_signal(barrier, inc=1, device_id=flat, device_id_type=LOGICAL)

    inputs = [
        pltpu.make_async_copy(source, target, input_sem.at[index])
        for index, (source, target) in enumerate(
            (
                (latitude_hbm, latitude_ref),
                (coefficients_hbm, coefficients),
                (pair_band_hbm, pair_band_ref),
                (cycle_hbm, cycle_ref),
                (factor_hbm, factor_ref),
                (order_hbm, order_ref),
            )
        )
    ]
    for_peers(signal, upper_half)
    for copy in inputs:
        copy.start()

    size = latitudes * entry
    part_row = lax.broadcasted_iota(jnp.int32, (entry, size), 0)
    offset = (lax.rem(part_row, own_fields) * parts + part_row // own_fields) * latitudes
    latitude_of = lax.broadcasted_iota(jnp.int32, (entry, size), 1) - offset

    def fill_pick(group):
        def one(pair, carry):
            pieces = []
            for side in range(2):
                number = group * GROUP + pair * 2 + side
                if band_rows == lanes * rows:
                    i, device = lax.div(number, devices), lax.rem(number, devices)
                    held = latitude_ref[device * rows + i]
                else:
                    i, device = lax.div(number, devices), lax.rem(number, devices)
                    local = lax.rem(device, lanes) * rows + i
                    row = (device // lanes) * band_rows + jnp.minimum(local, band_rows - 1)
                    held = jnp.where(local < band_rows, latitude_ref[row], -(1 << 20))
                pieces.append(jnp.where(latitude_of == held, 1.0, 0.0))
            start = pl.multiple_of(pair * 2 * entry, 2 * entry)
            pick[pl.ds(start, 2 * entry), :] = jnp.concatenate(pieces, axis=0).astype(jnp.bfloat16)
            return carry

        lax.fori_loop(0, GROUP // 2, one, 0, unroll=4)

    def flip(value):
        return pltpu.roll(value, main, 1)

    def down(value, count):
        count = count % value.shape[0]
        return pltpu.roll(value, count, 0) if count else value

    def places_of(value):
        row = lax.rem(lax.broadcasted_iota(jnp.int32, value.shape, 0), 8)
        return row, lax.broadcasted_iota(jnp.int32, value.shape, 1)

    def swap_parts(value):
        row, column = places_of(value)
        part = column // rest
        for bit in (1, 2, 4):
            row_set, part_set = (row // bit) % 2 == 1, (part // bit) % 2 == 1
            later = pltpu.roll(down(value, -bit), bit * rest, 1)
            earlier = pltpu.roll(down(value, bit), LANES - bit * rest, 1)
            value = jnp.where(
                row_set == part_set, value, jnp.where(row_set, earlier, later)
            )
        return value

    fifth = slice(2 * latitudes, 3 * latitudes)

    def rest_of_coefficients():
        total = jnp.zeros((latitudes, LANES), jnp.float32)
        column = lax.broadcasted_iota(jnp.int32, (latitudes, LANES), 1)
        blank = jnp.zeros((latitudes, LANES - slot_count), jnp.float32)
        for k in range(entry):
            held = coefficients[k % own_fields, k // own_fields].astype(jnp.float32)
            held = jnp.concatenate([held, blank], axis=1)
            held = pltpu.roll(held, (k * rest - main) % LANES, 1)
            inside = (column // rest == k) & (column % rest < slot_count - main)
            total = jnp.where(inside, held, total)
        return total.astype(jnp.bfloat16)

    if not packed:
        leaving[...] = jnp.zeros_like(leaving)
    inputs[0].wait()

    def gather(group, carry):
        fill_pick(group)
        if groups > 1:
            inputs_ready = coefficients[...]
        else:
            inputs[1].wait()
            inputs_ready = coefficients[...]
        picked = jnp.dot(
            pick[...], inputs_ready.reshape(size, slot_count), preferred_element_type=jnp.float32
        )
        if groups > 1:
            picked = picked.reshape(GROUP, entry, slot_count).astype(jnp.bfloat16)
            leaving[0, pl.ds(group * GROUP, GROUP), :, 0:slot_count] = picked
        else:
            if packed:
                tail = jnp.dot(
                    pick[:, fifth], rest_of_coefficients(), preferred_element_type=jnp.float32
                )
                blank = jnp.zeros((GROUP * entry, LANES - slot_count), jnp.float32)
                picked = jnp.concatenate([picked, blank], axis=1)
                row, column = places_of(picked)
                first = jnp.where(column < main, picked, flip(down(picked, -4)))
                picked = jnp.where(row < 4, first, jnp.where(row == 4, tail, 0.0))
                leaving[...] = picked.reshape(leaving.shape).astype(jnp.bfloat16)
            else:
                picked = picked.reshape(rows, devices, entry, slot_count).astype(jnp.bfloat16)
                leaving[:, :, :, 0:slot_count] = picked
        return carry

    if groups > 1:
        inputs[1].wait()
        lax.fori_loop(0, groups, gather, 0)
    else:
        gather(0, 0)

    inputs[2].wait()
    pair_band = pair_band_ref[...].reshape(1, half)
    source = lax.broadcasted_iota(jnp.int32, (half, half), 0)
    target = lax.broadcasted_iota(jnp.int32, (half, half), 1)
    earlier = jnp.where(source < target, 1.0, 0.0).astype(jnp.bfloat16)
    padded_bands = -(-bands // 16) * 16
    owner = lax.broadcasted_iota(jnp.int32, (padded_bands, half), 0) == pair_band
    counts = jnp.dot(
        jnp.where(owner, 1.0, 0.0).astype(jnp.bfloat16), earlier, preferred_element_type=jnp.float32
    )
    place = jnp.sum(jnp.where(owner, counts, 0.0), axis=0, keepdims=True)
    place = place.astype(jnp.int32)
    if packed:
        slot_of_pair = jnp.where(
            place < main,
            pair_band * main + place,
            bands * main + pair_band * rest + (place - main),
        )
    else:
        slot_of_pair = pair_band * slot_count + place
    slot = lax.broadcasted_iota(jnp.int32, (padded, half), 0)
    hot = jnp.where(slot == slot_of_pair, 1.0, 0.0).astype(jnp.bfloat16)
    number = lax.broadcasted_iota(jnp.int32, (half, 2 * LANES), 0) + 1
    upper = lax.broadcasted_iota(jnp.int32, (half, 2 * LANES), 1) < LANES
    digits = jnp.where(upper, number // 8, lax.rem(number, 8)).astype(jnp.float32)
    found = jnp.dot(hot, digits.astype(jnp.bfloat16), preferred_element_type=jnp.float32)
    wave_column[...] = found[:, :LANES] * 8.0 + found[:, LANES:]
    number = lax.broadcasted_iota(jnp.int32, (16, half), 1) + 1
    upper = lax.broadcasted_iota(jnp.int32, (16, half), 0) < 8
    digits = jnp.where(upper, number // 8, lax.rem(number, 8)).astype(jnp.float32)
    found = lax.dot_general(
        digits.astype(jnp.bfloat16),
        hot,
        (((1,), (1,)), ((), ())),
        preferred_element_type=jnp.float32,
    )
    ordinal = found[0:8] * 8.0 + found[8:16]
    wave_row = jnp.concatenate([ordinal - 1.0, waves - ordinal], axis=1)
    held_row = jnp.concatenate([ordinal, ordinal], axis=1) > 0.0

    inputs[3].wait()

    def tall(value, count):
        return jnp.concatenate([value] * (count // 8), axis=0)

    def length_of(i):
        row = jnp.minimum(lane * rows + i, band_rows - 1)
        n = cycle_ref[latitude_ref[band * band_rows + row]]
        length = jnp.full((1, 1), n, jnp.int32).astype(jnp.float32)
        return row, n, length, 1.0 / length

    def prepare_steps(i):
        row, n, length, inverse = length_of(i)
        step_ref[i, 0], step_ref[i, 1] = cos_sin(wave_row * float(CHUNK), length, inverse)
        step_ref[i, 2], step_ref[i, 3] = cos_sin(wave_row * float(2 * CHUNK), length, inverse)
        kept = jnp.where(held_row & (2.0 * wave_row < length), 1.0, 0.0)
        weight_ref[i] = kept

    def prepare_table(i, begin, end):
        row, n, length, inverse = length_of(i)

        places = lax.broadcasted_iota(jnp.int32, (8, CHUNK), 1).astype(jnp.float32)
        last_cosine, last_sine = cos_sin(places * float(waves - 1), length, inverse)

        def block(step, carry):
            start = pl.multiple_of(step * 16, 16)
            ordinal = wave_column[pl.ds(start, 16), :]
            for side in range(CHUNK // LANES):
                columns = slice(side * LANES, (side + 1) * LANES)
                place = lax.broadcasted_iota(jnp.int32, (16, LANES), 1) + side * LANES
                product = (ordinal - 1.0) * place.astype(jnp.float32)
                cosine, sine = cos_sin(product, length, inverse)
                top_cosine = tall(last_cosine[:, columns], 16)
                top_sine = tall(last_sine[:, columns], 16)
                pairs = (
                    (cosine, sine),
                    (
                        top_cosine * cosine + top_sine * sine,
                        top_sine * cosine - top_cosine * sine,
                    ),
                )
                for member, (cosine, sine) in enumerate(pairs):
                    at = pl.ds(member * padded + start, 16)
                    table[i, at, columns] = cosine.astype(jnp.bfloat16)
                    at = pl.ds(width + member * padded + start, 16)
                    table[i, at, columns] = (-sine).astype(jnp.bfloat16)
            return carry

        lax.fori_loop(begin, end, block, 0)

    blocks_all = padded // 16
    quarter = lax.div(own_plane * 4, planes)
    early = [jnp.where(quarter == 3, blocks_all // 2, blocks_all)]
    early += [jnp.where(quarter == 0, blocks_all, 0)] * (rows - 1)
    for i in range(rows):
        prepare_table(i, 0, early[i])
    inputs[4].wait()
    inputs[5].wait()

    pl.semaphore_wait(barrier, devices - 1)
    send_chunks(leaving, arrived, send_sem, recv_sem, every, upper_half)
    for j in range(1, lanes):
        factor_copy(j).start()
    cycles[:, block_of(lane)] = factor_ref[...]

    for i in range(rows):
        prepare_steps(i)
        prepare_table(i, early[i], blocks_all)
    for j in range(1, lanes):
        factor_copy(j).wait()
    for i in range(rows):
        chosen = lax.broadcasted_iota(jnp.int32, (band_rows, 1), 0) == length_of(i)[0]
        row_factor[i] = jnp.sum(
            jnp.where(chosen, cycles[...].astype(jnp.float32), 0.0), axis=0, keepdims=True
        )

    wait_chunks(leaving, arrived, send_sem, recv_sem, every)

    lane_index = lax.broadcasted_iota(jnp.int32, (stacked, LANES), 1)
    def compact_of(i):
        pieces = []
        for b in range(bands):
            piece = arrived[i, b * lanes : (b + 1) * lanes].astype(jnp.float32)
            pieces.append(piece.reshape(stacked, LANES))
        if packed:
            held = pieces
            row, column = places_of(held[0])
            columns = []
            for b in range(0, bands, 2):
                even, odd = held[b], held[b + 1]
                left = jnp.where(row < 4, even, flip(down(even, 4)))
                right = jnp.where(row < 4, flip(odd), down(odd, 4))
                columns.append(jnp.where(column < main, left, right))
            tail = jnp.zeros_like(held[0])
            for b in range(bands):
                tail = jnp.where(row == b, down(held[b], b - 4), tail)
            columns.append(swap_parts(tail))
            return jnp.dot(
                order_ref[...],
                jnp.concatenate(columns, axis=1).astype(jnp.bfloat16),
                preferred_element_type=jnp.float32,
            )
        by_part = jnp.dot(
            order_ref[...],
            jnp.concatenate(pieces, axis=1).astype(jnp.bfloat16),
            preferred_element_type=jnp.float32,
        )
        columns = [jnp.zeros((stacked, LANES), jnp.float32)] * (padded // LANES)
        for b in range(bands):
            first = b * slot_count
            turn = first % LANES
            piece = by_part[:, b * LANES : (b + 1) * LANES]
            piece = pltpu.roll(piece, turn, 1) if turn else piece
            for v in range(first // LANES, (first + slot_count - 1) // LANES + 1):
                begin = first - v * LANES
                if begin <= 0:
                    columns[v] = piece
                else:
                    columns[v] = jnp.where(lane_index >= begin, piece, columns[v])
        return jnp.concatenate(columns, axis=1)

    first_wave = jnp.where(wave_row == 0.0, 1.0, 2.0)

    def part_of(member, t):
        return (member * 2 + t) * fields

    for i in range(rows):
        row, n, length, inverse = length_of(i)
        norm = lax.rsqrt(length)
        live = tall(weight_ref[i] > 0.0, fields)
        scale = tall(first_wave, fields)
        state = []
        compact = compact_of(i)
        for t in range(2):
            held = jnp.concatenate(
                [compact[part_of(m, t) : part_of(m, t) + fields] for m in range(2)], axis=1
            )
            state.append(jnp.where(live, held * scale, 0.0))
        real, imag = state
        cosine, sine = tall(step_ref[i, 0], fields), tall(step_ref[i, 1], fields)
        real, imag = (
            jnp.concatenate([real, real * cosine - imag * sine], axis=0),
            jnp.concatenate([imag, real * sine + imag * cosine], axis=0),
        )
        cosine, sine = tall(step_ref[i, 2], 2 * fields), tall(step_ref[i, 3], 2 * fields)
        for h in range(chunks // 2):
            at = slice(2 * h * fields, 2 * (h + 1) * fields)
            lhs[i, at, 0:width] = real.astype(jnp.bfloat16)
            lhs[i, at, width : 2 * width] = imag.astype(jnp.bfloat16)
            if h < chunks // 2 - 1:
                real, imag = real * cosine - imag * sine, real * sine + imag * cosine

        found = jnp.dot(lhs[i], table[i], preferred_element_type=jnp.float32)
        for h in range(0, chunks, 2):
            pair = []
            for g in (h, h + 1):
                at = g * CHUNK + lax.broadcasted_iota(jnp.int32, (1, CHUNK), 1)
                value = found[g * fields : (g + 1) * fields]
                value = jnp.where(at < n, value * norm, 0.0).astype(jnp.bfloat16)
                grid_ref[i, :, g * CHUNK : (g + 1) * CHUNK] = value
                factor = row_factor[i, :, g * CHUNK : (g + 1) * CHUNK]
                pair.append(factor * value.astype(jnp.float32))
            product_ref[i, h * fields : (h + 2) * fields, :] = jnp.concatenate(
                pair, axis=0
            ).astype(jnp.bfloat16)
    def finish_packed(i):
        members = [finished[i, :, m * padded : (m + 1) * padded] for m in range(2)]
        by_lane = lax.dot_general(
            order_ref[...],
            jnp.concatenate(members, axis=0).astype(jnp.bfloat16),
            (((0,), (0,)), ((), ())),
            preferred_element_type=jnp.float32,
        )
        tail = swap_parts(by_lane[:, bands * main : bands * main + LANES])
        row, column = places_of(tail)
        for b in range(bands):
            held = by_lane[:, b // 2 * LANES : (b // 2 + 1) * LANES]
            if b % 2 == 0:
                piece = jnp.where(column < main, held, flip(down(held, -4)))
            else:
                piece = jnp.where(column < main, flip(held), down(held, -4))
            piece = jnp.where(row < 4, piece, down(tail, 4 - b))
            piece = piece.reshape(lanes, entry, LANES)
            result[i, b * lanes : (b + 1) * lanes] = piece.astype(jnp.bfloat16)
        send_chunks(result, returned, back_send_sem.at[i], back_recv_sem.at[i], i, True)

    def finish_row(i):
        if packed:
            return finish_packed(i)
        spread = []
        for b in range(bands):
            first = b * slot_count
            turn = first % LANES
            v = first // LANES
            members = []
            for member in range(2):
                base = member * padded + v * LANES
                piece = finished[i, :, base : base + LANES]
                piece = pltpu.roll(piece, LANES - turn, 1) if turn else piece
                if turn + slot_count > LANES:
                    after = finished[i, :, base + LANES : base + 2 * LANES]
                    after = pltpu.roll(after, LANES - turn, 1)
                    piece = jnp.where(lane_index[: 2 * fields] < LANES - turn, piece, after)
                members.append(piece)
            spread.append(jnp.concatenate(members, axis=0).astype(jnp.bfloat16))
        by_lane = lax.dot_general(
            order_ref[...],
            jnp.concatenate(spread, axis=1),
            (((0,), (0,)), ((), ())),
            preferred_element_type=jnp.float32,
        )
        for b in range(bands):
            piece = by_lane[:, b * LANES : (b + 1) * LANES].reshape(lanes, entry, LANES)
            result[i, b * lanes : (b + 1) * lanes] = piece.astype(jnp.bfloat16)
        send_chunks(result, returned, back_send_sem.at[i], back_recv_sem.at[i], i, True)

    for i in range(rows):
        row, n, length, inverse = length_of(i)
        norm = lax.rsqrt(length)
        left = product_ref[i]
        for c in range(width // CHUNK):
            columns = slice(c * CHUNK, (c + 1) * CHUNK)
            parts_found = []
            for t in range(2):
                right = table[i, t * width + c * CHUNK : t * width + (c + 1) * CHUNK, :]
                parts_found.append(
                    lax.dot_general(
                        left, right, (((1,), (1,)), ((), ())), preferred_element_type=jnp.float32
                    )
                )
            cosine = tall(step_ref[i, 0, :, columns], fields)
            sine = tall(step_ref[i, 1, :, columns], fields)
            last = slice((chunks - 1) * fields, chunks * fields)
            real, imag = parts_found[0][last], parts_found[1][last]
            for h in range(chunks - 2, -1, -1):
                at = slice(h * fields, (h + 1) * fields)
                real, imag = (
                    real * cosine + imag * sine + parts_found[0][at],
                    imag * cosine - real * sine + parts_found[1][at],
                )
            scale = tall(weight_ref[i, :, columns], fields) * norm
            for t, value in ((0, real), (1, imag)):
                finished[i, t * fields : (t + 1) * fields, columns] = value * scale
        finish_row(i)

    for i in range(rows):
        for j in range(1, lanes):
            grid_copy(i, j).start()
        blocks[lane, i] = grid_ref[i, :, block_of(lane)]

    for i in range(rows):
        for j in range(1, lanes):
            grid_copy(i, j).wait()
    if grid_out.ndim == 3:
        held = blocks[...].astype(jnp.float32).reshape(lanes * rows, fields, points)
        grid_out[...] = jnp.swapaxes(held, 0, 1).astype(jnp.bfloat16)
    else:
        grid_out[...] = blocks[...]
    for i in range(rows):
        wait_chunks(result, returned, back_send_sem.at[i], back_recv_sem.at[i], i)

    def place_group(group):
        if groups > 1:
            held = returned[0, pl.ds(group * GROUP, GROUP)].astype(jnp.float32)
        else:
            held = returned[...].astype(jnp.float32)
        held = held.reshape(GROUP * entry, LANES)
        if packed:
            row, column = places_of(held)
            held = jnp.where(row < 5, held, 0.0)
            spread = jnp.where(row < 4, held, flip(down(held, 4)))
            across = (((0,), (0,)), ((), ()))
            first = lax.dot_general(
                pick[...], spread.astype(jnp.bfloat16), across, preferred_element_type=jnp.float32
            )
            tail = lax.dot_general(
                pick[:, fifth],
                held.astype(jnp.bfloat16),
                across,
                preferred_element_type=jnp.float32,
            )
            tails = [None] * entry
            for k in range(entry):
                at = (k % own_fields) * parts + k // own_fields
                tails[at] = pltpu.roll(tail, (main - k * rest) % LANES, 1)
            row, column = places_of(first)
            return jnp.where(column < main, first, jnp.concatenate(tails, axis=0))
        held = held.astype(jnp.bfloat16)
        return lax.dot_general(
            pick[...], held, (((0,), (0,)), ((), ())), preferred_element_type=jnp.float32
        )

    if groups == 1:
        placed = place_group(0)
    else:

        def add(group, total):
            fill_pick(group)
            return total + place_group(group)

        placed = lax.fori_loop(0, groups, add, jnp.zeros((size, LANES), jnp.float32))
    placed = placed[:, :slot_count].reshape(own_fields, parts, latitudes, slot_count)
    tendencies[...] = placed.astype(jnp.bfloat16)


def round_trip(coefficients, cycle_length, row_latitude, pair_band, factor, order, bands, lanes):
    devices = bands * lanes
    own_fields, parts, latitudes, slot_count = coefficients.shape
    fields = own_fields * lanes
    band_rows, points = factor.shape
    rows = -(-band_rows // lanes)
    entry = parts * own_fields
    padded = -(-bands * slot_count // LANES) * LANES
    width = 2 * padded
    chunks = lanes * points // CHUNK
    exchange = (rows, devices, entry, LANES)
    grid_shape = (lanes, rows, fields, points)
    if lanes * rows == band_rows and band_rows % 8 == 0 and fields % 8 == 0:
        grid_shape = (fields, band_rows, points)
    bf16, f32 = jnp.bfloat16, jnp.float32
    hbm = pl.BlockSpec(memory_space=pltpu.MemorySpace.HBM)
    return pl.pallas_call(
        functools.partial(round_kernel, bands, lanes),
        in_specs=[hbm] * 6,
        out_specs=[pl.BlockSpec(memory_space=pltpu.VMEM)] * 2,
        scratch_shapes=[
            pltpu.VMEM((lanes, rows, fields, points), bf16),
            pltpu.VMEM(coefficients.shape, bf16),
            pltpu.SMEM(cycle_length.shape, jnp.int32),
            pltpu.SMEM(row_latitude.shape, jnp.int32),
            pltpu.VMEM(pair_band.shape, jnp.int32),
            pltpu.VMEM(factor.shape, bf16),
            pltpu.VMEM(order.shape, bf16),
            pltpu.VMEM((GROUP * entry, latitudes * entry), bf16),
            pltpu.VMEM(exchange, bf16),
            pltpu.VMEM(exchange, bf16),
            pltpu.VMEM(exchange, bf16),
            pltpu.VMEM(exchange, bf16),
            pltpu.VMEM((band_rows, lanes * points), bf16),
            pltpu.VMEM((rows, fields, lanes * points), bf16),
            pltpu.VMEM((rows, 2 * width, CHUNK), bf16),
            pltpu.VMEM((rows, chunks * fields, 2 * width), bf16),
            pltpu.VMEM((rows, chunks * fields, CHUNK), bf16),
            pltpu.VMEM((rows, 1, lanes * points), f32),
            pltpu.VMEM((padded, LANES), f32),
            pltpu.VMEM((rows, 4, 8, width), f32),
            pltpu.VMEM((rows, 8, width), f32),
            pltpu.VMEM((rows, 2 * fields, width), f32),
        ]
        + [pltpu.SemaphoreType.DMA((6,))]
        + [pltpu.SemaphoreType.DMA] * 2
        + [pltpu.SemaphoreType.DMA((rows,))] * 2
        + [pltpu.SemaphoreType.DMA((lanes,))] * 2
        + [pltpu.SemaphoreType.DMA((rows, lanes))] * 2,
        out_shape=[
            jax.ShapeDtypeStruct(grid_shape, bf16),
            jax.ShapeDtypeStruct(coefficients.shape, bf16),
        ],
        compiler_params=pltpu.CompilerParams(
            collective_id=0, has_side_effects=True, vmem_limit_bytes=40 << 20
        ),
    )(
        *[
            pltpu.with_memory_space_constraint(array, pltpu.MemorySpace.HBM)
            for array in (coefficients, cycle_length, row_latitude, pair_band, factor, order)
        ]
    )


def write_kernel(*refs):
    count = (len(refs) - 1) // 2
    copies = [
        pltpu.make_async_copy(refs[index], refs[count + index], refs[-1].at[index])
        for index in range(count)
    ]
    for copy in copies:
        copy.start()
    for copy in copies:
        copy.wait()


def write_outputs(*arrays):
    return pl.pallas_call(
        write_kernel,
        in_specs=[pl.BlockSpec(memory_space=pltpu.VMEM)] * len(arrays),
        out_specs=[pl.BlockSpec(memory_space=pl.ANY)] * len(arrays),
        out_shape=[jax.ShapeDtypeStruct(array.shape, array.dtype) for array in arrays],
        scratch_shapes=[pltpu.SemaphoreType.DMA((len(arrays),))],
        compiler_params=pltpu.CompilerParams(vmem_limit_bytes=16 << 20),
    )(*arrays)


def on_device(coefficients, cycle_length, row_latitude, pair_band, gridpoint_factor):
    bands, lanes = lax.axis_size("band"), lax.axis_size("lon")
    own_fields, slot_count, parts, latitudes = coefficients.shape
    band_rows, points = gridpoint_factor.shape
    fields = own_fields * lanes
    own_rows = -(-band_rows // lanes)
    stacked = lanes * parts * own_fields
    places = np.arange(stacked).reshape(lanes, parts, own_fields)
    places = places.transpose(1, 0, 2).reshape(-1)
    order = jnp.asarray(places[:, None] == np.arange(stacked)[None, :], dtype=jnp.bfloat16)
    grid, placed = round_trip(
        jnp.transpose(coefficients, (0, 2, 3, 1)),
        cycle_length,
        row_latitude,
        pair_band,
        gridpoint_factor,
        order,
        bands,
        lanes,
    )
    if grid.ndim == 3:
        grid, placed = write_outputs(grid, placed)
    else:
        grid = grid.reshape(lanes * own_rows, fields, points)[:band_rows]
        grid = jnp.transpose(grid, (1, 0, 2))
    return (grid, jnp.transpose(placed, (0, 3, 1, 2)))


def solution(mesh):
    return jax.shard_map(
        on_device,
        mesh=mesh,
        in_specs=(P("lon", "band", None, None), P(), P(), P(), P("band", "lon")),
        out_specs=(P(None, "band", "lon"), P("lon", "band", None, None)),
        check_vma=False,
    )
```

```python
import functools
import math

import jax
import jax.numpy as jnp
import numpy as np
from jax import lax
from jax.experimental import pallas as pl
from jax.experimental.pallas import tpu as pltpu
from jax.sharding import PartitionSpec as P

TWO_PI = 2.0 * math.pi
LANES = 128
CHUNK = 256
GROUP = 64
MESH = pl.DeviceIdType.MESH
LOGICAL = pl.DeviceIdType.LOGICAL


def cos_sin(product, length, inverse):
    turns = jnp.floor(product * inverse + 0.5)
    half = (product - turns * length) * (inverse * (0.5 * TWO_PI))
    square = half * half
    sine = jnp.full_like(half, -1.0 / math.factorial(11))
    for order in (9, 7, 5, 3, 1):
        sine = sine * square + (-1.0) ** (order // 2) / math.factorial(order)
    sine = sine * half
    cosine = jnp.full_like(half, 1.0 / math.factorial(12))
    for order in (10, 8, 6, 4, 2, 0):
        cosine = cosine * square + (-1.0) ** (order // 2) / math.factorial(order)
    return 1.0 - 2.0 * sine * sine, 2.0 * sine * cosine


def round_kernel(
    bands,
    lanes,
    coefficients_hbm,
    cycle_hbm,
    latitude_hbm,
    pair_band_hbm,
    factor_hbm,
    order_hbm,
    grid_out,
    tendencies,
    blocks,
    coefficients,
    cycle_ref,
    latitude_ref,
    pair_band_ref,
    factor_ref,
    order_ref,
    pick,
    leaving,
    arrived,
    result,
    returned,
    cycles,
    grid_ref,
    table,
    lhs,
    product_ref,
    row_factor,
    wave_column,
    step_ref,
    weight_ref,
    finished,
    input_sem,
    send_sem,
    recv_sem,
    back_send_sem,
    back_recv_sem,
    factor_send_sem,
    factor_recv_sem,
    grid_send_sem,
    grid_recv_sem,
):
    band, lane = lax.axis_index("band"), lax.axis_index("lon")
    me = band * lanes + lane
    devices = bands * lanes
    band_rows, points = factor_ref.shape
    rows, fields = grid_ref.shape[0], grid_ref.shape[1]
    own_fields, parts, latitudes, slot_count = coefficients.shape
    half = pair_band_ref.shape[-1]
    waves = 2 * half
    padded = wave_column.shape[0]
    width = 2 * padded
    cycle_points = lanes * points
    chunks = cycle_points // CHUNK
    entry = parts * own_fields
    entries = devices * rows
    stacked = entry * lanes
    groups = entries // GROUP
    every = slice(0, rows)
    main, rest = LANES // 2, LANES // 8
    packed = bands == 8 and entry == 8 and groups == 1 and main < slot_count <= main + rest
    wire = slice(0, 6) if packed else slice(0, entry)
    unroll = devices <= 32

    plane = 2 * lanes
    planes = devices // plane
    own_plane = lax.div(band, 2)
    own_place = me - own_plane * plane
    upper_half = own_plane >= planes - planes // 2

    def for_peers(act, first_planes):
        def place_at(turn):
            place = own_place + turn
            return jnp.where(place >= plane, place - plane, place)

        def facing(shift):
            level = own_plane + shift
            level = jnp.where(level >= planes, level - planes, level)
            act(level * plane + own_place)

        def others(step, turn):
            level = jnp.where(first_planes, step, planes - 1 - step)
            act(level * plane + place_at(turn))

        if unroll:
            for shift in range(1, planes):
                facing(shift)
            for step in range(planes):
                for turn in range(1, plane):
                    others(step, turn)
        else:
            lax.fori_loop(1, planes, lambda shift, carry: (facing(shift), carry)[1], 0)

            def one(step, carry):
                return lax.fori_loop(1, plane, lambda turn, c: (others(step, turn), c)[1], carry)

            lax.fori_loop(0, planes, one, 0)

    def block_of(index):
        return pl.ds(pl.multiple_of(index * points, LANES), points)

    def send_chunks(source, target, sent, received, row, first_planes):
        def send(flat):
            pltpu.make_async_remote_copy(
                src_ref=source.at[row, flat, wire],
                dst_ref=target.at[row, me, wire],
                send_sem=sent,
                recv_sem=received,
                device_id=flat,
                device_id_type=LOGICAL,
            ).start()

        for_peers(send, first_planes)
        target[row, me] = source[row, me]

    def wait_chunks(source, target, sent, received, row):
        pltpu.make_async_remote_copy(
            src_ref=source.at[row, pl.ds(0, devices - 1), wire],
            dst_ref=target.at[row, pl.ds(0, devices - 1), wire],
            send_sem=sent,
            recv_sem=received,
            device_id={"band": band, "lon": lane},
            device_id_type=MESH,
        ).wait()

    def factor_copy(j):
        return pltpu.make_async_remote_copy(
            src_ref=factor_ref,
            dst_ref=cycles.at[:, block_of(lane)],
            send_sem=factor_send_sem.at[j],
            recv_sem=factor_recv_sem.at[j],
            device_id={"lon": lax.rem(lane + j, lanes)},
            device_id_type=MESH,
        )

    def grid_copy(i, j):
        other = lax.rem(lane + j, lanes)
        return pltpu.make_async_remote_copy(
            src_ref=grid_ref.at[i, :, block_of(other)],
            dst_ref=blocks.at[lane, i],
            send_sem=grid_send_sem.at[i, j],
            recv_sem=grid_recv_sem.at[i, j],
            device_id={"lon": other},
            device_id_type=MESH,
        )

    barrier = pltpu.get_barrier_semaphore()

    def signal(flat):
        pl.semaphore_signal(barrier, inc=1, device_id=flat, device_id_type=LOGICAL)

    inputs = [
        pltpu.make_async_copy(source, target, input_sem.at[index])
        for index, (source, target) in enumerate(
            (
                (latitude_hbm, latitude_ref),
                (coefficients_hbm, coefficients),
                (pair_band_hbm, pair_band_ref),
                (cycle_hbm, cycle_ref),
                (factor_hbm, factor_ref),
                (order_hbm, order_ref),
            )
        )
    ]
    for_peers(signal, upper_half)
    for copy in inputs:
        copy.start()

    size = latitudes * entry
    part_row = lax.broadcasted_iota(jnp.int32, (entry, size), 0)
    offset = (lax.rem(part_row, own_fields) * parts + part_row // own_fields) * latitudes
    latitude_of = lax.broadcasted_iota(jnp.int32, (entry, size), 1) - offset

    def fill_pick(group):
        def one(pair, carry):
            pieces = []
            for side in range(2):
                number = group * GROUP + pair * 2 + side
                if band_rows == lanes * rows:
                    i, device = lax.div(number, devices), lax.rem(number, devices)
                    held = latitude_ref[device * rows + i]
                else:
                    i, device = lax.div(number, devices), lax.rem(number, devices)
                    local = lax.rem(device, lanes) * rows + i
                    row = (device // lanes) * band_rows + jnp.minimum(local, band_rows - 1)
                    held = jnp.where(local < band_rows, latitude_ref[row], -(1 << 20))
                pieces.append(jnp.where(latitude_of == held, 1.0, 0.0))
            start = pl.multiple_of(pair * 2 * entry, 2 * entry)
            pick[pl.ds(start, 2 * entry), :] = jnp.concatenate(pieces, axis=0).astype(jnp.bfloat16)
            return carry

        lax.fori_loop(0, GROUP // 2, one, 0, unroll=4)

    def flip(value):
        return pltpu.roll(value, main, 1)

    def down(value, count):
        count = count % value.shape[0]
        return pltpu.roll(value, count, 0) if count else value

    def places_of(value):
        row = lax.rem(lax.broadcasted_iota(jnp.int32, value.shape, 0), 8)
        return row, lax.broadcasted_iota(jnp.int32, value.shape, 1)

    def swap_parts(value):
        row, column = places_of(value)
        part = column // rest
        for bit in (1, 2, 4):
            row_set, part_set = (row // bit) % 2 == 1, (part // bit) % 2 == 1
            later = pltpu.roll(down(value, -bit), bit * rest, 1)
            earlier = pltpu.roll(down(value, bit), LANES - bit * rest, 1)
            value = jnp.where(
                row_set == part_set, value, jnp.where(row_set, earlier, later)
            )
        return value

    fifth = slice(2 * latitudes, 3 * latitudes)

    def rest_of_coefficients():
        total = jnp.zeros((latitudes, LANES), jnp.float32)
        column = lax.broadcasted_iota(jnp.int32, (latitudes, LANES), 1)
        blank = jnp.zeros((latitudes, LANES - slot_count), jnp.float32)
        for k in range(entry):
            held = coefficients[k % own_fields, k // own_fields].astype(jnp.float32)
            held = jnp.concatenate([held, blank], axis=1)
            held = pltpu.roll(held, (k * rest - main) % LANES, 1)
            inside = (column // rest == k) & (column % rest < slot_count - main)
            total = jnp.where(inside, held, total)
        return total.astype(jnp.bfloat16)

    if not packed:
        leaving[...] = jnp.zeros_like(leaving)
    inputs[0].wait()

    def gather(group, carry):
        fill_pick(group)
        if groups > 1:
            inputs_ready = coefficients[...]
        else:
            inputs[1].wait()
            inputs_ready = coefficients[...]
        picked = jnp.dot(
            pick[...], inputs_ready.reshape(size, slot_count), preferred_element_type=jnp.float32
        )
        if groups > 1:
            picked = picked.reshape(GROUP, entry, slot_count).astype(jnp.bfloat16)
            leaving[0, pl.ds(group * GROUP, GROUP), :, 0:slot_count] = picked
        else:
            if packed:
                tail = jnp.dot(
                    pick[:, fifth], rest_of_coefficients(), preferred_element_type=jnp.float32
                )
                blank = jnp.zeros((GROUP * entry, LANES - slot_count), jnp.float32)
                picked = jnp.concatenate([picked, blank], axis=1)
                row, column = places_of(picked)
                first = jnp.where(column < main, picked, flip(down(picked, -4)))
                picked = jnp.where(row < 4, first, jnp.where(row == 4, tail, 0.0))
                leaving[...] = picked.reshape(leaving.shape).astype(jnp.bfloat16)
            else:
                picked = picked.reshape(rows, devices, entry, slot_count).astype(jnp.bfloat16)
                leaving[:, :, :, 0:slot_count] = picked
        return carry

    if groups > 1:
        inputs[1].wait()
        lax.fori_loop(0, groups, gather, 0)
    else:
        gather(0, 0)

    inputs[2].wait()
    pair_band = pair_band_ref[...].reshape(1, half)
    source = lax.broadcasted_iota(jnp.int32, (half, half), 0)
    target = lax.broadcasted_iota(jnp.int32, (half, half), 1)
    earlier = jnp.where(source < target, 1.0, 0.0).astype(jnp.bfloat16)
    padded_bands = -(-bands // 16) * 16
    owner = lax.broadcasted_iota(jnp.int32, (padded_bands, half), 0) == pair_band
    counts = jnp.dot(
        jnp.where(owner, 1.0, 0.0).astype(jnp.bfloat16), earlier, preferred_element_type=jnp.float32
    )
    place = jnp.sum(jnp.where(owner, counts, 0.0), axis=0, keepdims=True)
    place = place.astype(jnp.int32)
    if packed:
        slot_of_pair = jnp.where(
            place < main,
            pair_band * main + place,
            bands * main + pair_band * rest + (place - main),
        )
    else:
        slot_of_pair = pair_band * slot_count + place
    slot = lax.broadcasted_iota(jnp.int32, (padded, half), 0)
    hot = jnp.where(slot == slot_of_pair, 1.0, 0.0).astype(jnp.bfloat16)
    number = lax.broadcasted_iota(jnp.int32, (half, 2 * LANES), 0) + 1
    upper = lax.broadcasted_iota(jnp.int32, (half, 2 * LANES), 1) < LANES
    digits = jnp.where(upper, number // 8, lax.rem(number, 8)).astype(jnp.float32)
    found = jnp.dot(hot, digits.astype(jnp.bfloat16), preferred_element_type=jnp.float32)
    wave_column[...] = found[:, :LANES] * 8.0 + found[:, LANES:]
    number = lax.broadcasted_iota(jnp.int32, (16, half), 1) + 1
    upper = lax.broadcasted_iota(jnp.int32, (16, half), 0) < 8
    digits = jnp.where(upper, number // 8, lax.rem(number, 8)).astype(jnp.float32)
    found = lax.dot_general(
        digits.astype(jnp.bfloat16),
        hot,
        (((1,), (1,)), ((), ())),
        preferred_element_type=jnp.float32,
    )
    ordinal = found[0:8] * 8.0 + found[8:16]
    wave_row = jnp.concatenate([ordinal - 1.0, waves - ordinal], axis=1)
    held_row = jnp.concatenate([ordinal, ordinal], axis=1) > 0.0

    inputs[3].wait()

    def tall(value, count):
        return jnp.concatenate([value] * (count // 8), axis=0)

    def length_of(i):
        row = jnp.minimum(lane * rows + i, band_rows - 1)
        n = cycle_ref[latitude_ref[band * band_rows + row]]
        length = jnp.full((1, 1), n, jnp.int32).astype(jnp.float32)
        return row, n, length, 1.0 / length

    def prepare_steps(i):
        row, n, length, inverse = length_of(i)
        step_ref[i, 0], step_ref[i, 1] = cos_sin(wave_row * float(CHUNK), length, inverse)
        step_ref[i, 2], step_ref[i, 3] = cos_sin(wave_row * float(2 * CHUNK), length, inverse)
        kept = jnp.where(held_row & (2.0 * wave_row < length), 1.0, 0.0)
        weight_ref[i] = kept

    def prepare_table(i, begin, end):
        row, n, length, inverse = length_of(i)

        places = lax.broadcasted_iota(jnp.int32, (8, CHUNK), 1).astype(jnp.float32)
        last_cosine, last_sine = cos_sin(places * float(waves - 1), length, inverse)

        def block(step, carry):
            start = pl.multiple_of(step * 16, 16)
            ordinal = wave_column[pl.ds(start, 16), :]
            for side in range(CHUNK // LANES):
                columns = slice(side * LANES, (side + 1) * LANES)
                place = lax.broadcasted_iota(jnp.int32, (16, LANES), 1) + side * LANES
                product = (ordinal - 1.0) * place.astype(jnp.float32)
                cosine, sine = cos_sin(product, length, inverse)
                top_cosine = tall(last_cosine[:, columns], 16)
                top_sine = tall(last_sine[:, columns], 16)
                pairs = (
                    (cosine, sine),
                    (
                        top_cosine * cosine + top_sine * sine,
                        top_sine * cosine - top_cosine * sine,
                    ),
                )
                for member, (cosine, sine) in enumerate(pairs):
                    at = pl.ds(member * padded + start, 16)
                    table[i, at, columns] = cosine.astype(jnp.bfloat16)
                    at = pl.ds(width + member * padded + start, 16)
                    table[i, at, columns] = (-sine).astype(jnp.bfloat16)
            return carry

        lax.fori_loop(begin, end, block, 0)

    blocks_all = padded // 16
    quarter = lax.div(own_plane * 4, planes)
    early = [jnp.where(quarter == 3, blocks_all // 2, blocks_all)]
    early += [jnp.where(quarter == 0, blocks_all, 0)] * (rows - 1)
    for i in range(rows):
        prepare_table(i, 0, early[i])
    inputs[4].wait()
    inputs[5].wait()

    pl.semaphore_wait(barrier, devices - 1)
    send_chunks(leaving, arrived, send_sem, recv_sem, every, upper_half)
    for j in range(1, lanes):
        factor_copy(j).start()
    cycles[:, block_of(lane)] = factor_ref[...]

    for i in range(rows):
        prepare_steps(i)
        prepare_table(i, early[i], blocks_all)
    for j in range(1, lanes):
        factor_copy(j).wait()
    for i in range(rows):
        chosen = lax.broadcasted_iota(jnp.int32, (band_rows, 1), 0) == length_of(i)[0]
        row_factor[i] = jnp.sum(
            jnp.where(chosen, cycles[...].astype(jnp.float32), 0.0), axis=0, keepdims=True
        )

    wait_chunks(leaving, arrived, send_sem, recv_sem, every)

    lane_index = lax.broadcasted_iota(jnp.int32, (stacked, LANES), 1)
    def compact_of(i):
        pieces = []
        for b in range(bands):
            piece = arrived[i, b * lanes : (b + 1) * lanes].astype(jnp.float32)
            pieces.append(piece.reshape(stacked, LANES))
        if packed:
            held = pieces
            row, column = places_of(held[0])
            columns = []
            for b in range(0, bands, 2):
                even, odd = held[b], held[b + 1]
                left = jnp.where(row < 4, even, flip(down(even, 4)))
                right = jnp.where(row < 4, flip(odd), down(odd, 4))
                columns.append(jnp.where(column < main, left, right))
            tail = jnp.zeros_like(held[0])
            for b in range(bands):
                tail = jnp.where(row == b, down(held[b], b - 4), tail)
            columns.append(swap_parts(tail))
            return jnp.dot(
                order_ref[...],
                jnp.concatenate(columns, axis=1).astype(jnp.bfloat16),
                preferred_element_type=jnp.float32,
            )
        by_part = jnp.dot(
            order_ref[...],
            jnp.concatenate(pieces, axis=1).astype(jnp.bfloat16),
            preferred_element_type=jnp.float32,
        )
        columns = [jnp.zeros((stacked, LANES), jnp.float32)] * (padded // LANES)
        for b in range(bands):
            first = b * slot_count
            turn = first % LANES
            piece = by_part[:, b * LANES : (b + 1) * LANES]
            piece = pltpu.roll(piece, turn, 1) if turn else piece
            for v in range(first // LANES, (first + slot_count - 1) // LANES + 1):
                begin = first - v * LANES
                if begin <= 0:
                    columns[v] = piece
                else:
                    columns[v] = jnp.where(lane_index >= begin, piece, columns[v])
        return jnp.concatenate(columns, axis=1)

    first_wave = jnp.where(wave_row == 0.0, 1.0, 2.0)

    def part_of(member, t):
        return (member * 2 + t) * fields

    for i in range(rows):
        row, n, length, inverse = length_of(i)
        norm = lax.rsqrt(length)
        live = tall(weight_ref[i] > 0.0, fields)
        scale = tall(first_wave, fields)
        state = []
        compact = compact_of(i)
        for t in range(2):
            held = jnp.concatenate(
                [compact[part_of(m, t) : part_of(m, t) + fields] for m in range(2)], axis=1
            )
            state.append(jnp.where(live, held * scale, 0.0))
        real, imag = state
        cosine, sine = tall(step_ref[i, 0], fields), tall(step_ref[i, 1], fields)
        real, imag = (
            jnp.concatenate([real, real * cosine - imag * sine], axis=0),
            jnp.concatenate([imag, real * sine + imag * cosine], axis=0),
        )
        cosine, sine = tall(step_ref[i, 2], 2 * fields), tall(step_ref[i, 3], 2 * fields)
        for h in range(chunks // 2):
            at = slice(2 * h * fields, 2 * (h + 1) * fields)
            lhs[i, at, 0:width] = real.astype(jnp.bfloat16)
            lhs[i, at, width : 2 * width] = imag.astype(jnp.bfloat16)
            if h < chunks // 2 - 1:
                real, imag = real * cosine - imag * sine, real * sine + imag * cosine

        found = jnp.dot(lhs[i], table[i], preferred_element_type=jnp.float32)
        for h in range(0, chunks, 2):
            pair = []
            for g in (h, h + 1):
                at = g * CHUNK + lax.broadcasted_iota(jnp.int32, (1, CHUNK), 1)
                value = found[g * fields : (g + 1) * fields]
                value = jnp.where(at < n, value * norm, 0.0).astype(jnp.bfloat16)
                grid_ref[i, :, g * CHUNK : (g + 1) * CHUNK] = value
                factor = row_factor[i, :, g * CHUNK : (g + 1) * CHUNK]
                pair.append(factor * value.astype(jnp.float32))
            product_ref[i, h * fields : (h + 2) * fields, :] = jnp.concatenate(
                pair, axis=0
            ).astype(jnp.bfloat16)
    def finish_packed(i):
        members = [finished[i, :, m * padded : (m + 1) * padded] for m in range(2)]
        by_lane = lax.dot_general(
            order_ref[...],
            jnp.concatenate(members, axis=0).astype(jnp.bfloat16),
            (((0,), (0,)), ((), ())),
            preferred_element_type=jnp.float32,
        )
        tail = swap_parts(by_lane[:, bands * main : bands * main + LANES])
        row, column = places_of(tail)
        for b in range(bands):
            held = by_lane[:, b // 2 * LANES : (b // 2 + 1) * LANES]
            if b % 2 == 0:
                piece = jnp.where(column < main, held, flip(down(held, -4)))
            else:
                piece = jnp.where(column < main, flip(held), down(held, -4))
            piece = jnp.where(row < 4, piece, down(tail, 4 - b))
            piece = piece.reshape(lanes, entry, LANES)
            result[i, b * lanes : (b + 1) * lanes] = piece.astype(jnp.bfloat16)

    def finish_row(i):
        if packed:
            return finish_packed(i)
        spread = []
        for b in range(bands):
            first = b * slot_count
            turn = first % LANES
            v = first // LANES
            members = []
            for member in range(2):
                base = member * padded + v * LANES
                piece = finished[i, :, base : base + LANES]
                piece = pltpu.roll(piece, LANES - turn, 1) if turn else piece
                if turn + slot_count > LANES:
                    after = finished[i, :, base + LANES : base + 2 * LANES]
                    after = pltpu.roll(after, LANES - turn, 1)
                    piece = jnp.where(lane_index[: 2 * fields] < LANES - turn, piece, after)
                members.append(piece)
            spread.append(jnp.concatenate(members, axis=0).astype(jnp.bfloat16))
        by_lane = lax.dot_general(
            order_ref[...],
            jnp.concatenate(spread, axis=1),
            (((0,), (0,)), ((), ())),
            preferred_element_type=jnp.float32,
        )
        for b in range(bands):
            piece = by_lane[:, b * LANES : (b + 1) * LANES].reshape(lanes, entry, LANES)
            result[i, b * lanes : (b + 1) * lanes] = piece.astype(jnp.bfloat16)

    for i in range(rows):
        row, n, length, inverse = length_of(i)
        norm = lax.rsqrt(length)
        left = product_ref[i]
        for c in range(width // CHUNK):
            columns = slice(c * CHUNK, (c + 1) * CHUNK)
            parts_found = []
            for t in range(2):
                right = table[i, t * width + c * CHUNK : t * width + (c + 1) * CHUNK, :]
                parts_found.append(
                    lax.dot_general(
                        left, right, (((1,), (1,)), ((), ())), preferred_element_type=jnp.float32
                    )
                )
            cosine = tall(step_ref[i, 0, :, columns], fields)
            sine = tall(step_ref[i, 1, :, columns], fields)
            last = slice((chunks - 1) * fields, chunks * fields)
            real, imag = parts_found[0][last], parts_found[1][last]
            for h in range(chunks - 2, -1, -1):
                at = slice(h * fields, (h + 1) * fields)
                real, imag = (
                    real * cosine + imag * sine + parts_found[0][at],
                    imag * cosine - real * sine + parts_found[1][at],
                )
            scale = tall(weight_ref[i, :, columns], fields) * norm
            for t, value in ((0, real), (1, imag)):
                finished[i, t * fields : (t + 1) * fields, columns] = value * scale
        finish_row(i)

    send_chunks(result, returned, back_send_sem, back_recv_sem, every, True)
    for i in range(rows):
        for j in range(1, lanes):
            grid_copy(i, j).start()
        blocks[lane, i] = grid_ref[i, :, block_of(lane)]

    for i in range(rows):
        for j in range(1, lanes):
            grid_copy(i, j).wait()
    if grid_out.ndim == 3:
        held = blocks[...].astype(jnp.float32).reshape(lanes * rows, fields, points)
        grid_out[...] = jnp.swapaxes(held, 0, 1).astype(jnp.bfloat16)
    else:
        grid_out[...] = blocks[...]
    wait_chunks(result, returned, back_send_sem, back_recv_sem, every)

    def place_group(group):
        if groups > 1:
            held = returned[0, pl.ds(group * GROUP, GROUP)].astype(jnp.float32)
        else:
            held = returned[...].astype(jnp.float32)
        held = held.reshape(GROUP * entry, LANES)
        if packed:
            row, column = places_of(held)
            held = jnp.where(row < 5, held, 0.0)
            spread = jnp.where(row < 4, held, flip(down(held, 4)))
            across = (((0,), (0,)), ((), ()))
            first = lax.dot_general(
                pick[...], spread.astype(jnp.bfloat16), across, preferred_element_type=jnp.float32
            )
            tail = lax.dot_general(
                pick[:, fifth],
                held.astype(jnp.bfloat16),
                across,
                preferred_element_type=jnp.float32,
            )
            tails = [None] * entry
            for k in range(entry):
                at = (k % own_fields) * parts + k // own_fields
                tails[at] = pltpu.roll(tail, (main - k * rest) % LANES, 1)
            row, column = places_of(first)
            return jnp.where(column < main, first, jnp.concatenate(tails, axis=0))
        held = held.astype(jnp.bfloat16)
        return lax.dot_general(
            pick[...], held, (((0,), (0,)), ((), ())), preferred_element_type=jnp.float32
        )

    if groups == 1:
        placed = place_group(0)
    else:

        def add(group, total):
            fill_pick(group)
            return total + place_group(group)

        placed = lax.fori_loop(0, groups, add, jnp.zeros((size, LANES), jnp.float32))
    placed = placed[:, :slot_count].reshape(own_fields, parts, latitudes, slot_count)
    tendencies[...] = placed.astype(jnp.bfloat16)


def round_trip(coefficients, cycle_length, row_latitude, pair_band, factor, order, bands, lanes):
    devices = bands * lanes
    own_fields, parts, latitudes, slot_count = coefficients.shape
    fields = own_fields * lanes
    band_rows, points = factor.shape
    rows = -(-band_rows // lanes)
    entry = parts * own_fields
    padded = -(-bands * slot_count // LANES) * LANES
    width = 2 * padded
    chunks = lanes * points // CHUNK
    exchange = (rows, devices, entry, LANES)
    grid_shape = (lanes, rows, fields, points)
    if lanes * rows == band_rows and band_rows % 8 == 0 and fields % 8 == 0:
        grid_shape = (fields, band_rows, points)
    bf16, f32 = jnp.bfloat16, jnp.float32
    hbm = pl.BlockSpec(memory_space=pltpu.MemorySpace.HBM)
    return pl.pallas_call(
        functools.partial(round_kernel, bands, lanes),
        in_specs=[hbm] * 6,
        out_specs=[pl.BlockSpec(memory_space=pltpu.VMEM)] * 2,
        scratch_shapes=[
            pltpu.VMEM((lanes, rows, fields, points), bf16),
            pltpu.VMEM(coefficients.shape, bf16),
            pltpu.SMEM(cycle_length.shape, jnp.int32),
            pltpu.SMEM(row_latitude.shape, jnp.int32),
            pltpu.VMEM(pair_band.shape, jnp.int32),
            pltpu.VMEM(factor.shape, bf16),
            pltpu.VMEM(order.shape, bf16),
            pltpu.VMEM((GROUP * entry, latitudes * entry), bf16),
            pltpu.VMEM(exchange, bf16),
            pltpu.VMEM(exchange, bf16),
            pltpu.VMEM(exchange, bf16),
            pltpu.VMEM(exchange, bf16),
            pltpu.VMEM((band_rows, lanes * points), bf16),
            pltpu.VMEM((rows, fields, lanes * points), bf16),
            pltpu.VMEM((rows, 2 * width, CHUNK), bf16),
            pltpu.VMEM((rows, chunks * fields, 2 * width), bf16),
            pltpu.VMEM((rows, chunks * fields, CHUNK), bf16),
            pltpu.VMEM((rows, 1, lanes * points), f32),
            pltpu.VMEM((padded, LANES), f32),
            pltpu.VMEM((rows, 4, 8, width), f32),
            pltpu.VMEM((rows, 8, width), f32),
            pltpu.VMEM((rows, 2 * fields, width), f32),
        ]
        + [pltpu.SemaphoreType.DMA((6,))]
        + [pltpu.SemaphoreType.DMA] * 4
        + [pltpu.SemaphoreType.DMA((lanes,))] * 2
        + [pltpu.SemaphoreType.DMA((rows, lanes))] * 2,
        out_shape=[
            jax.ShapeDtypeStruct(grid_shape, bf16),
            jax.ShapeDtypeStruct(coefficients.shape, bf16),
        ],
        compiler_params=pltpu.CompilerParams(
            collective_id=0, has_side_effects=True, vmem_limit_bytes=40 << 20
        ),
    )(
        *[
            pltpu.with_memory_space_constraint(array, pltpu.MemorySpace.HBM)
            for array in (coefficients, cycle_length, row_latitude, pair_band, factor, order)
        ]
    )


def write_kernel(*refs):
    count = (len(refs) - 1) // 2
    copies = [
        pltpu.make_async_copy(refs[index], refs[count + index], refs[-1].at[index])
        for index in range(count)
    ]
    for copy in copies:
        copy.start()
    for copy in copies:
        copy.wait()


def write_outputs(*arrays):
    return pl.pallas_call(
        write_kernel,
        in_specs=[pl.BlockSpec(memory_space=pltpu.VMEM)] * len(arrays),
        out_specs=[pl.BlockSpec(memory_space=pl.ANY)] * len(arrays),
        out_shape=[jax.ShapeDtypeStruct(array.shape, array.dtype) for array in arrays],
        scratch_shapes=[pltpu.SemaphoreType.DMA((len(arrays),))],
        compiler_params=pltpu.CompilerParams(vmem_limit_bytes=16 << 20),
    )(*arrays)


def on_device(coefficients, cycle_length, row_latitude, pair_band, gridpoint_factor):
    bands, lanes = lax.axis_size("band"), lax.axis_size("lon")
    own_fields, slot_count, parts, latitudes = coefficients.shape
    band_rows, points = gridpoint_factor.shape
    fields = own_fields * lanes
    own_rows = -(-band_rows // lanes)
    stacked = lanes * parts * own_fields
    places = np.arange(stacked).reshape(lanes, parts, own_fields)
    places = places.transpose(1, 0, 2).reshape(-1)
    order = jnp.asarray(places[:, None] == np.arange(stacked)[None, :], dtype=jnp.bfloat16)
    grid, placed = round_trip(
        jnp.transpose(coefficients, (0, 2, 3, 1)),
        cycle_length,
        row_latitude,
        pair_band,
        gridpoint_factor,
        order,
        bands,
        lanes,
    )
    if grid.ndim == 3:
        grid, placed = write_outputs(grid, placed)
    else:
        grid = grid.reshape(lanes * own_rows, fields, points)[:band_rows]
        grid = jnp.transpose(grid, (1, 0, 2))
    return (grid, jnp.transpose(placed, (0, 3, 1, 2)))


def solution(mesh):
    return jax.shard_map(
        on_device,
        mesh=mesh,
        in_specs=(P("lon", "band", None, None), P(), P(), P(), P("band", "lon")),
        out_specs=(P(None, "band", "lon"), P("lon", "band", None, None)),
        check_vma=False,
    )
```
